512 devices in a mesh: lat: 16 (over y, core), lev: 32 (over z, x).
Axes of the slice: x: 4, y: 8, z: 8, core: 2. Of those that a mesh axis runs over, the one named last changes fastest.
Arguments:
- fields: float32 [4, 128, 128, 1152], P(None, 'lev', 'lat'), may hold values from -6 to 6
- winds: float32 [2, 128, 128, 1152], P(None, 'lev', 'lat'), may hold values from -0.3 to 0.3
- remap_weight: bfloat16 [128, 128], replicated, may hold values from -0.5 to 0.5
- w_first: bfloat16 [512, 512], replicated, may hold values from -0.25 to 0.25
- w_second: bfloat16 [512, 512], replicated, may hold values from -0.25 to 0.25
- w_third: bfloat16 [512, 512], replicated, may hold values from -0.25 to 0.25
- lon_counts: int32 [16, 32], P('lat'), may hold values from 1 to 128, 1152 in all within a row
- group_list: int32 [16, 6], replicated, may hold values from 0 to 127, as said below
Outputs:
- columns_out: bfloat16 [4, 128, 128, 4096], P(None, None, 'lat', 'lev')
The draws below stay inside these ranges and needn't reach their ends.
Inputs may be any that keep to these rules, and one draw needn't show every extreme that they name: `lon_counts`: each row sums to 1152, and its largest entry is exactly 128. `group_list`: row p lists in ascending order the 6 latitude rows whose columns owner p (index p of lat) processes; no row appears twice; every row j with j // 8 equal to 8 appears; at most 1 row of one owner's list have the same j // 8, and some owner has exactly 1 such rows.
All inputs are finite; a program needn't handle non-finite values.
Results may differ from the reference program's by a relative error of at most 0.0053.
Values may be sent and summed in bfloat16 or wider, within the bound.
A program may use at most 64 MiB of HBM per device.

```python
import math
import jax
import jax.numpy as jnp
import numpy as np
from jax import lax

F = 4
NLEV = 128
HID = 512
LAT_DEV = 8
NLON = 1152
NLAT = 128
CAP = 128
ROWS_PER = 6
FN = 512
N_LAT = 16
N_LEV = 32


def draw_group_list(key, part):
    band_count = NLAT // LAT_DEV
    middle = band_count // 2
    needed = band_count * ROWS_PER - LAT_DEV
    picked = jax.random.permutation(key, NLAT - LAT_DEV)[:needed].astype(jnp.int32)
    others = picked + LAT_DEV * (picked >= middle * LAT_DEV).astype(jnp.int32)
    central = middle * LAT_DEV + jnp.arange(LAT_DEV, dtype=jnp.int32)
    listed = jnp.sort(jnp.concatenate([central, others]))
    dealt_rows = listed.reshape(ROWS_PER, band_count).T
    owner_order = jax.random.permutation(jax.random.fold_in(key, 7), band_count)
    inverse = jnp.argsort(owner_order)
    return dealt_rows[inverse].astype(jnp.int32)


def block_scale(key, shape, shards, low, top_value):
    gain = 1.0
    for dim, shards_of in shards:
        heights = jax.random.uniform(jax.random.fold_in(jax.random.fold_in(key, 6), dim), (shards_of,), jnp.float32, low / len(shards), top_value / len(shards))
        gain = gain * jnp.repeat(jnp.exp(heights), shape[dim] // shards_of).reshape((-1,) + (1,) * (len(shape) - 1 - dim))
    return gain


def profile(amount, total, most, lean):
    loads = [(1 << 20) // math.isqrt(grade ** lean) + 1 for grade in range(2, amount + 1)]
    spare, holding = total - most - (amount - 1), [1] * (amount - 1)
    while spare > 0:
        movable = [i for i in range(amount - 1) if holding[i] < most]
        mass, budget = sum([loads[i] for i in movable]), spare
        for i in movable:
            extra = min(most - holding[i], max(1, budget * loads[i] // mass), spare)
            holding[i] = holding[i] + extra
            spare = spare - extra
    return np.array([most] + holding)


def ragged_sizes(key, amount, total, bound, skew):
    if amount == 2:
        one = jax.random.randint(key, (), max(1, total - bound), min(bound, total - 1) + 1)
        return jnp.stack([one, total - one])
    sizes = jnp.asarray(profile(amount, total, bound, skew), jnp.int32)
    pairs = (amount - 1) // 2
    donor, taker = sizes[1:1 + 2 * pairs:2], sizes[2:2 + 2 * pairs:2]
    slack = jnp.minimum(donor - 1, bound - taker)
    shifted = jax.random.randint(jax.random.fold_in(key, 1), (pairs,), 0, 1 << 20) % (slack + 1)
    sizes = sizes.at[1:1 + 2 * pairs:2].set(donor - shifted).at[2:2 + 2 * pairs:2].set(taker + shifted)
    return sizes[jax.random.permutation(jax.random.fold_in(key, 2), amount)]


def scatter_about(own_key, extent, scale, limit, pieces=(), held_as=jnp.bfloat16):
    array = jax.random.normal(own_key, extent, jnp.float32) * scale
    if len(pieces) > 0:
        array = block_scale(own_key, extent, pieces, -0.22, 0.18) * array
    return jnp.clip(array, min=-limit, max=limit).astype(held_as)


def setup_inputs(seed: int = 0) -> dict:
    key_list = jax.random.split(jax.random.key(seed), 9)
    return {
        "fields": scatter_about(key_list[0], (F, NLEV, NLAT, NLON), 1.0, 6.0, ((1, 32), (2, 16)), jnp.float32),
        "winds": jnp.clip(jax.random.uniform(key_list[1], (2, NLEV, NLAT, NLON), jnp.float32, -0.3, 0.3) * block_scale(key_list[1], (2, NLEV, NLAT, NLON), ((1, 32), (2, 16)), -0.4, 0.0), -0.3, 0.3),
        "remap_weight": scatter_about(key_list[2], (NLEV, NLEV), NLEV ** -0.5, 0.5),
        "w_first": scatter_about(key_list[3], (FN, HID), FN ** -0.5, 0.25),
        "w_second": scatter_about(key_list[4], (HID, HID), HID ** -0.5, 0.25),
        "w_third": scatter_about(key_list[5], (HID, FN), HID ** -0.5, 0.25),
        "lon_counts": jax.vmap(lambda own: ragged_sizes(own, N_LEV, NLON, CAP, 2))(jax.random.split(key_list[6], N_LAT)).reshape((N_LAT, N_LEV)).astype(jnp.int32),
        "group_list": draw_group_list(jax.random.fold_in(key_list[8], 71), 0),
    }


DIFFUSION = 0.15


def flux_divergence(values, east_wind, north_wind, first_row, total_rows):
    inner_count = values.shape[-2] - 2
    face_flux = 0.25 * (north_wind[..., :-1, :] + north_wind[..., 1:, :]) * (values[..., :-1, :] + values[..., 1:, :])
    face_flux = face_flux - DIFFUSION * (values[..., 1:, :] - values[..., :-1, :])
    faces = first_row + jnp.arange(inner_count + 1, dtype=jnp.int32)
    keep_face = ((faces >= 1) & (faces <= total_rows - 1)).astype(jnp.float32)[:, None]
    face_flux = face_flux * keep_face
    inner = values[..., 1:-1, :]
    inner_wind = east_wind[..., 1:-1, :]
    west_values = jnp.roll(inner, 1, axis=-1)
    west_wind = jnp.roll(inner_wind, 1, axis=-1)
    side_flux = 0.25 * (west_wind + inner_wind) * (west_values + inner) - DIFFUSION * (inner - west_values)
    return -(face_flux[..., 1:, :] - face_flux[..., :-1, :]) - (jnp.roll(side_flux, -1, axis=-1) - side_flux)


def pad_rows(values):
    return jnp.pad(values, ((0, 0), (1, 1), (0, 0)))


def convect(columns, w_first, w_second, w_third):
    pattern = (((0,), (0,)), ((), ()))
    hidden_one = jax.nn.silu(lax.dot_general(w_first, columns, pattern, preferred_element_type=jnp.float32)).astype(jnp.bfloat16)
    hidden_two = jax.nn.silu(lax.dot_general(w_second, hidden_one, pattern, preferred_element_type=jnp.float32)).astype(jnp.bfloat16)
    return lax.dot_general(w_third, hidden_two, pattern, preferred_element_type=jnp.float32).astype(jnp.bfloat16)


def reference(fields, winds, remap_weight, w_first, w_second, w_third, lon_counts, group_list):
    east_padded = pad_rows(winds[0])
    north_padded = pad_rows(winds[1])

    def advect_field(field_values):
        predicted = field_values + flux_divergence(pad_rows(field_values), east_padded, north_padded, 0, NLAT)
        return 0.5 * (field_values + predicted + flux_divergence(pad_rows(predicted), east_padded, north_padded, 0, NLAT))

    advected = lax.map(advect_field, fields)
    rounded = advected.astype(jnp.bfloat16)
    weight_wide = remap_weight.astype(jnp.float32)

    def remap_field(block):
        values = block.astype(jnp.float32)
        return values + jnp.einsum("mn,nrc->mrc", weight_wide, values, precision=lax.Precision.HIGHEST)

    remapped = lax.map(remap_field, rounded)
    listed = jnp.any(group_list.reshape(-1)[None, :] == jnp.arange(NLAT, dtype=jnp.int32)[:, None], axis=1)
    lon_start = jnp.cumsum(lon_counts, axis=1) - lon_counts
    offsets = jnp.arange(CAP, dtype=jnp.int32)
    by_rows = remapped.transpose(2, 0, 1, 3)

    def one_row(row_index):
        row_values = lax.dynamic_index_in_dim(by_rows, row_index, 0, keepdims=False)
        features = row_values.astype(jnp.bfloat16).reshape(F * NLEV, NLON)
        tendency = lax.cond(listed[row_index],
                            lambda: convect(features, w_first, w_second, w_third),
                            lambda: jnp.zeros((F * NLEV, NLON), jnp.bfloat16))
        updated = (row_values + tendency.astype(jnp.float32).reshape(F, NLEV, NLON)).astype(jnp.bfloat16)
        band_number = row_index // LAT_DEV
        lon_index = lon_start[band_number][:, None] + offsets[None, :]
        in_range = offsets[None, :] < lon_counts[band_number][:, None]
        picked = jnp.take(updated, jnp.minimum(lon_index, NLON - 1).reshape(-1).astype(jnp.int32), axis=2)
        return jnp.where(in_range.reshape(-1)[None, None, :], picked, jnp.zeros_like(picked))

    rows_out = lax.map(one_row, jnp.arange(NLAT, dtype=jnp.int32))
    return rows_out.transpose(1, 2, 0, 3)
```

```python
import functools

import jax
import jax.numpy as jnp
from jax import lax
from jax.experimental import pallas as pl
from jax.experimental.pallas import tpu as pltpu
from jax.sharding import PartitionSpec as P

DIFFUSION = 0.15
SLOT = 128
MESH = pl.DeviceIdType.MESH
BF = jnp.bfloat16
F32 = jnp.float32


def kernel(
    n_lat, n_lev, x_size, lev_total,
    cnt_ref, grp_ref, fields_hbm, winds_hbm, rw_hbm, w1_hbm, w2_hbm, w3_hbm,
    out_ref,
    up_buf, down_buf, lo_buf, hi_buf,
    tracer, wind_in, sown, ew, nw, ah, bh, ag, bg, pred, adv,
    send, recv,
    rw_in, w1_in, w2_in, w3_in, mix, w1t, w2t, w3t, done,
    halo_send, halo_recv, send_sem, recv_sem, load_sem, in_sem,
):
    rows, fields_count = 8, 4
    group = send.shape[2]
    levels = group // fields_count
    halves = group // 8
    lon = fields_hbm.shape[1]
    feats = n_lev * group
    chunks = ((2, 3), (4, 5), (0, 1), (6, 7))

    lat = lax.axis_index("lat")
    me = lax.axis_index("lev")
    up, down = lax.rem(lat + 1, n_lat), lax.rem(lat + n_lat - 1, n_lat)
    z_size = n_lev // x_size
    my_z, my_x = me // x_size, lax.rem(me, x_size)

    def peer_of(i):
        step, dx = i // x_size, lax.rem(i, x_size) + 1
        dz = z_size // 2 + (1 - 2 * lax.rem(step, 2)) * ((step + 1) // 2)
        return lax.rem(my_z + dz, z_size) * x_size + lax.rem(my_x + dx, x_size)

    barrier = pltpu.get_barrier_semaphore()
    for other in (up, down):
        pl.semaphore_signal(barrier, inc=1, device_id={"lat": other}, device_id_type=MESH)

    @pl.loop(0, n_lev - 1)
    def _(i):
        pl.semaphore_signal(barrier, inc=1, device_id={"lev": peer_of(i)}, device_id_type=MESH)

    tiles = lon // SLOT
    columns = [slice(t * SLOT, (t + 1) * SLOT) for t in range(tiles)]
    inputs = []
    for t, part in enumerate(columns):
        cut = pl.ds(t * SLOT, SLOT)
        inputs.append(pltpu.make_async_copy(fields_hbm.at[:, cut], tracer.at[t], in_sem.at[0, t]))
        inputs.append(pltpu.make_async_copy(winds_hbm.at[:, cut], wind_in.at[t], in_sem.at[1, t]))
    for copy in inputs:
        copy.start()

    loads = [
        pltpu.make_async_copy(src, dst, load_sem.at[i])
        for i, (src, dst) in enumerate(
            ((rw_hbm, rw_in), (w1_hbm, w1_in), (w2_hbm, w2_in), (w3_hbm, w3_in))
        )
    ]
    for load in loads:
        load.start()

    def twice(x):
        return jnp.concatenate([x, x], axis=0)

    for t, part in enumerate(columns):
        inputs[2 * t].wait()
        inputs[2 * t + 1].wait()
        for r in range(rows):
            for h in range(halves):
                sown[r, h, :, part] = tracer[t, pl.ds(h * 8 * rows + r, 8, stride=rows), :]
            for which, kept in ((0, ew), (1, nw)):
                kept[r, :, part] = twice(wind_in[t, pl.ds(which * levels * rows + r, levels, stride=rows), :])
    for buf, far, near, order in ((up_buf, 6, 7, (6, 7)), (down_buf, 1, 0, (0, 1))):
        for k, r in enumerate(order):
            for h in range(halves):
                buf[k * halves + h] = sown[r, h]
        buf[2 * halves] = jnp.concatenate([ew[near, :levels], nw[near, :levels]], axis=0)
        buf[2 * halves + 1] = nw[far]

    def value(r, h):
        if r < 0:
            return lo_buf[(r + 2) * halves + h]
        if r >= rows:
            return hi_buf[(r - rows) * halves + h]
        return sown[r, h]

    def east(r):
        if r < 0:
            return twice(lo_buf[2 * halves, :levels])
        if r >= rows:
            return twice(hi_buf[2 * halves, :levels])
        return ew[r]

    def north(r):
        if r == -2:
            return lo_buf[2 * halves + 1]
        if r == -1:
            return twice(lo_buf[2 * halves, levels:])
        if r == rows:
            return twice(hi_buf[2 * halves, levels:])
        if r == rows + 1:
            return hi_buf[2 * halves + 1]
        return nw[r]

    def make_side(r):
        u = east(r)
        c = 0.25 * (pltpu.roll(u, 1, axis=1) + u)
        ah[r + 1] = c + DIFFUSION
        bh[r + 1] = c - DIFFUSION

    def make_face(j):
        c = 0.25 * (north(j - 1) + north(j))
        a, b = c + DIFFUSION, c - DIFFUSION
        if j == 0:
            keep = jnp.where(lat > 0, 1.0, 0.0).astype(F32)
            a, b = a * keep, b * keep
        if j == rows:
            keep = jnp.where(lat < n_lat - 1, 1.0, 0.0).astype(F32)
            a, b = a * keep, b * keep
        ag[j + 1] = a
        bg[j + 1] = b

    def sweep(get, span, emit):
        for h in range(halves):
            face = None
            for r in span:
                here = get(r, h)
                if face is None:
                    face = ag[r + 1] * get(r - 1, h) + bg[r + 1] * here
                after = ag[r + 2] * here + bg[r + 2] * get(r + 1, h)
                side = ah[r + 1] * pltpu.roll(here, 1, axis=1) + bh[r + 1] * here
                change = (face - after) + (side - pltpu.roll(side, lon - 1, axis=1))
                emit(r, h, here, change)
                face = after

    def first_step(r, h, here, change):
        pred[r + 1, h] = here + change

    def second_step(r, h, here, change):
        result = 0.5 * (value(r, h) + here + change)
        for t, part in enumerate(columns):
            adv[t, r, h] = result[:, part]

    def guess(r, h):
        return pred[r + 1, h]

    lane = lax.broadcasted_iota(jnp.int32, (8, SLOT), 1)

    def compact(c):
        def body(k, start):
            tile = start >> 7
            shift = start & (SLOT - 1)
            back = (SLOT - shift) & (SLOT - 1)
            take = lane < SLOT - shift
            for i, r in enumerate(chunks[c]):
                parts = []
                for h in range(halves):
                    a = pltpu.roll(adv[tile, r, h], back, axis=1)
                    b = pltpu.roll(adv[tile + 1, r, h], back, axis=1)
                    parts.append(jnp.where(take, a, b))
                send[c, k, :, i * SLOT : (i + 1) * SLOT] = jnp.concatenate(parts, axis=0).astype(BF)
            return start + cnt_ref[0, k]

        lax.fori_loop(0, n_lev, body, jnp.int32(0), unroll=4)

    def ship(c):
        @pl.loop(0, n_lev - 1)
        def _(i):
            peer = peer_of(i)
            pltpu.make_async_remote_copy(
                src_ref=send.at[c, peer],
                dst_ref=recv.at[c, me],
                send_sem=send_sem.at[c],
                recv_sem=recv_sem.at[c],
                device_id={"lev": peer},
                device_id_type=MESH,
            ).start()

        pltpu.make_async_copy(send.at[c, me], recv.at[c, me], recv_sem.at[c]).start()

    adv[tiles] = jnp.zeros(adv.shape[1:], F32)
    for r in range(rows):
        make_side(r)
    for j in range(1, rows):
        make_face(j)
    sweep(value, range(1, 7), first_step)
    sweep(guess, range(2, 6), second_step)
    compact(0)

    pl.semaphore_wait(barrier, n_lev + 1)

    halos = [
        pltpu.make_async_remote_copy(
            src_ref=src,
            dst_ref=dst,
            send_sem=halo_send.at[i],
            recv_sem=halo_recv.at[i],
            device_id={"lat": other},
            device_id_type=MESH,
        )
        for i, (src, dst, other) in enumerate(((up_buf, lo_buf, up), (down_buf, hi_buf, down)))
    ]
    for halo in halos:
        halo.start()
    ship(0)
    compact(1)
    ship(1)

    for halo in halos:
        halo.wait()
    for r in (-1, rows):
        make_side(r)
    for j in (-1, 0, rows, rows + 1):
        make_face(j)
    sweep(value, (-1, 0), first_step)
    sweep(value, (7, 8), first_step)
    sweep(guess, (0, 1), second_step)
    compact(2)
    ship(2)
    sweep(guess, (6, 7), second_step)
    compact(3)
    ship(3)

    def iota(shape, dim):
        return lax.broadcasted_iota(jnp.int32, shape, dim)

    def hot(mask):
        return jnp.where(mask, 1.0, 0.0).astype(BF)

    def field_of(p):
        return lax.rem(p // levels, fields_count)

    def level_of(p):
        return (p // group) * levels + lax.rem(p, levels)

    def dot(a, b, dims=((1,), (0,))):
        return lax.dot_general(a, b, (dims, ((), ())), preferred_element_type=F32)

    for load in loads:
        load.wait()
    p_col = iota((feats, feats), 0)
    order = hot(field_of(p_col) * lev_total + level_of(p_col) == iota((feats, feats), 1))
    expand = hot(level_of(iota((feats, lev_total), 0)) == iota((feats, lev_total), 1))
    spread = dot(dot(expand, rw_in[...]).astype(BF), expand, ((1,), (1,)))
    same = field_of(iota((feats, feats), 0)) == field_of(iota((feats, feats), 1))
    mix[...] = jnp.where(same, spread, 0.0).astype(BF)
    w1t[...] = dot(order, w1_in[...]).T.astype(BF)
    w2t[...] = w2_in[...].astype(F32).T.astype(BF)
    w3t[...] = dot(order, w3_in[...].astype(F32).T.astype(BF)).astype(BF)

    def silu(x):
        return x / (1.0 + jnp.exp(-x))

    for c, pair in enumerate(chunks):
        pltpu.make_async_copy(recv.at[c], recv.at[c], recv_sem.at[c]).wait()
        block = recv[c].reshape(feats, 2 * SLOT)
        remapped = block.astype(F32) + dot(mix[...], block)
        hidden = silu(dot(w1t[...], remapped.astype(BF))).astype(BF)
        hidden = silu(dot(w2t[...], hidden)).astype(BF)
        tendency = dot(w3t[...], hidden).astype(BF).astype(F32)
        for i, r in enumerate(pair):
            hit = jnp.max(jnp.where(grp_ref[...] == lat * rows + r, 1.0, 0.0), keepdims=True)
            part = slice(i * SLOT, (i + 1) * SLOT)
            done[pl.ds(r, feats, stride=rows), :] = remapped[:, part] + hit * tendency[:, part]

    keep = lane < cnt_ref[0, me]

    @pl.loop(0, n_lev)
    def _(src):
        for q in range(group):
            tile = done[pl.ds(pl.multiple_of((src * group + q) * rows, rows), rows), :]
            out_ref[q // levels, src * levels + q % levels] = jnp.where(keep, tile, 0.0).astype(BF)

    for c in range(len(chunks)):
        sent = send.at[c, pl.ds(0, n_lev - 1)]
        pltpu.make_async_copy(sent, sent, send_sem.at[c]).wait()


def shards(n_lat, n_lev, x_size, fields, winds, remap_weight, w_first, w_second, w_third, lon_counts, group_list):
    field_count, levels, rows, lon = fields.shape
    group = field_count * levels
    lev_total = remap_weight.shape[0]
    feats = group * n_lev
    hid = w_first.shape[1]
    halves = group // 8
    hbm = pl.BlockSpec(memory_space=pltpu.HBM)
    vmem = pl.BlockSpec(memory_space=pltpu.VMEM)
    plane = (8, lon)
    halo = (2 * halves + 2,) + plane
    return pl.pallas_call(
        functools.partial(kernel, n_lat, n_lev, x_size, lev_total),
        out_shape=jax.ShapeDtypeStruct((field_count, lev_total, rows, SLOT), BF),
        in_specs=[pl.BlockSpec(memory_space=pltpu.SMEM), vmem, hbm, hbm, hbm, hbm, hbm, hbm],
        out_specs=vmem,
        scratch_shapes=[
            pltpu.VMEM(halo, F32), pltpu.VMEM(halo, F32),
            pltpu.VMEM(halo, F32), pltpu.VMEM(halo, F32),
            pltpu.VMEM((lon // SLOT, group * rows, SLOT), F32),
            pltpu.VMEM((lon // SLOT, 2 * levels * rows, SLOT), F32),
            pltpu.VMEM((rows, halves) + plane, F32),
            pltpu.VMEM((rows,) + plane, F32), pltpu.VMEM((rows,) + plane, F32),
            pltpu.VMEM((rows + 2,) + plane, F32), pltpu.VMEM((rows + 2,) + plane, F32),
            pltpu.VMEM((rows + 3,) + plane, F32), pltpu.VMEM((rows + 3,) + plane, F32),
            pltpu.VMEM((rows + 2, halves) + plane, F32),
            pltpu.VMEM((lon // SLOT + 1, rows, halves, 8, SLOT), F32),
            pltpu.VMEM((4, n_lev, group, 2 * SLOT), BF),
            pltpu.VMEM((4, n_lev, group, 2 * SLOT), BF),
            pltpu.VMEM(remap_weight.shape, BF), pltpu.VMEM(w_first.shape, BF),
            pltpu.VMEM(w_second.shape, BF), pltpu.VMEM(w_third.shape, BF),
            pltpu.VMEM((feats, feats), BF), pltpu.VMEM((hid, feats), BF),
            pltpu.VMEM((hid, hid), BF), pltpu.VMEM((feats, hid), BF),
            pltpu.VMEM((feats * rows, SLOT), F32),
            pltpu.SemaphoreType.DMA((2,)), pltpu.SemaphoreType.DMA((2,)),
            pltpu.SemaphoreType.DMA((4,)), pltpu.SemaphoreType.DMA((4,)),
            pltpu.SemaphoreType.DMA((4,)), pltpu.SemaphoreType.DMA((2, lon // SLOT)),
        ],
        compiler_params=pltpu.CompilerParams(
            collective_id=0, has_side_effects=True, vmem_limit_bytes=48 * 1024 * 1024
        ),
    )(
        lon_counts, group_list, fields.reshape(group * rows, lon), winds.reshape(2 * levels * rows, lon),
        remap_weight, w_first, w_second, w_third,
    )


def solution(mesh):
    n_lat, n_lev = mesh.shape["lat"], mesh.shape["lev"]
    in_specs = (
        P(None, "lev", "lat", None),
        P(None, "lev", "lat", None),
        P(), P(), P(), P(),
        P("lat", None),
        P(),
    )
    return jax.shard_map(
        functools.partial(shards, n_lat, n_lev, 4),
        mesh=mesh,
        in_specs=in_specs,
        out_specs=P(None, None, "lat", "lev"),
        check_vma=False,
    )
```

```python
import functools

import jax
import jax.numpy as jnp
from jax import lax
from jax.experimental import pallas as pl
from jax.experimental.pallas import tpu as pltpu
from jax.sharding import PartitionSpec as P

DIFFUSION = 0.15
SLOT = 128
LIMIT = 48000000
MESH = pl.DeviceIdType.MESH
BF = jnp.bfloat16
F32 = jnp.float32


def kernel(
    n_lat, n_lev, x_size, lev_total,
    cnt_hbm, grp_hbm, fields_hbm, winds_hbm, rw_hbm, w1_hbm, w2_hbm, w3_hbm,
    out_ref,
    up_buf, down_buf, lo_buf, hi_buf,
    tracer, wind_in, sown, ew, nw, ah, bh, ag, bg, pred, adv,
    send, recv,
    rw_in, w1_in, w2_in, w3_in, mix, w1t, w2t, w3t, done,
    halo_send, halo_recv, send_sem, recv_sem, load_sem, in_sem, cnt_ref, grp_ref,
):
    rows, fields_count = 8, 4
    group = send.shape[2]
    levels = group // fields_count
    halves = group // 8
    lon = fields_hbm.shape[1]
    feats = n_lev * group
    chunks = ((2, 3), (4, 5), (0, 1), (6, 7))

    lat = lax.axis_index("lat")
    me = lax.axis_index("lev")
    up, down = lax.rem(lat + 1, n_lat), lax.rem(lat + n_lat - 1, n_lat)
    z_size = n_lev // x_size
    my_z, my_x = me // x_size, lax.rem(me, x_size)

    def peer_of(i):
        step, dx = i // x_size, lax.rem(i, x_size) + 1
        dz = z_size // 2 + (1 - 2 * lax.rem(step, 2)) * ((step + 1) // 2)
        return lax.rem(my_z + dz, z_size) * x_size + lax.rem(my_x + dx, x_size)

    barrier = pltpu.get_barrier_semaphore()
    for other in (up, down):
        pl.semaphore_signal(barrier, inc=1, device_id={"lat": other}, device_id_type=MESH)

    @pl.loop(0, n_lev - 1)
    def _(i):
        pl.semaphore_signal(barrier, inc=1, device_id={"lev": peer_of(i)}, device_id_type=MESH)

    tiles = lon // SLOT
    columns = [slice(t * SLOT, (t + 1) * SLOT) for t in range(tiles)]
    inputs = []
    for t, part in enumerate(columns):
        cut = pl.ds(t * SLOT, SLOT)
        inputs.append(pltpu.make_async_copy(fields_hbm.at[:, cut], tracer.at[t], in_sem.at[0, t]))
        inputs.append(pltpu.make_async_copy(winds_hbm.at[:, cut], wind_in.at[t], in_sem.at[1, t]))
    for copy in inputs:
        copy.start()

    loads = [
        pltpu.make_async_copy(src, dst, load_sem.at[i])
        for i, (src, dst) in enumerate(
            ((cnt_hbm, cnt_ref), (grp_hbm, grp_ref), (rw_hbm, rw_in), (w1_hbm, w1_in), (w2_hbm, w2_in), (w3_hbm, w3_in))
        )
    ]
    for load in loads:
        load.start()

    def twice(x):
        return jnp.concatenate([x, x], axis=0)

    for t, part in enumerate(columns):
        inputs[2 * t].wait()
        inputs[2 * t + 1].wait()
        for r in range(rows):
            for h in range(halves):
                sown[r, h, :, part] = tracer[t, pl.ds(h * 8 * rows + r, 8, stride=rows), :]
            for which, kept in ((0, ew), (1, nw)):
                kept[r, :, part] = twice(wind_in[t, pl.ds(which * levels * rows + r, levels, stride=rows), :])
    for buf, far, near, order in ((up_buf, 6, 7, (6, 7)), (down_buf, 1, 0, (0, 1))):
        for k, r in enumerate(order):
            for h in range(halves):
                buf[k * halves + h] = sown[r, h]
        buf[2 * halves] = jnp.concatenate([ew[near, :levels], nw[near, :levels]], axis=0)
        buf[2 * halves + 1] = nw[far]

    def value(r, h):
        if r < 0:
            return lo_buf[(r + 2) * halves + h]
        if r >= rows:
            return hi_buf[(r - rows) * halves + h]
        return sown[r, h]

    def east(r):
        if r < 0:
            return twice(lo_buf[2 * halves, :levels])
        if r >= rows:
            return twice(hi_buf[2 * halves, :levels])
        return ew[r]

    def north(r):
        if r == -2:
            return lo_buf[2 * halves + 1]
        if r == -1:
            return twice(lo_buf[2 * halves, levels:])
        if r == rows:
            return twice(hi_buf[2 * halves, levels:])
        if r == rows + 1:
            return hi_buf[2 * halves + 1]
        return nw[r]

    def make_side(r):
        u = east(r)
        c = 0.25 * (pltpu.roll(u, 1, axis=1) + u)
        ah[r + 1] = c + DIFFUSION
        bh[r + 1] = c - DIFFUSION

    def make_face(j):
        c = 0.25 * (north(j - 1) + north(j))
        a, b = c + DIFFUSION, c - DIFFUSION
        if j == 0:
            keep = jnp.where(lat > 0, 1.0, 0.0).astype(F32)
            a, b = a * keep, b * keep
        if j == rows:
            keep = jnp.where(lat < n_lat - 1, 1.0, 0.0).astype(F32)
            a, b = a * keep, b * keep
        ag[j + 1] = a
        bg[j + 1] = b

    def sweep(get, span, emit):
        for h in range(halves):
            face = None
            for r in span:
                here = get(r, h)
                if face is None:
                    face = ag[r + 1] * get(r - 1, h) + bg[r + 1] * here
                after = ag[r + 2] * here + bg[r + 2] * get(r + 1, h)
                side = ah[r + 1] * pltpu.roll(here, 1, axis=1) + bh[r + 1] * here
                change = (face - after) + (side - pltpu.roll(side, lon - 1, axis=1))
                emit(r, h, here, change)
                face = after

    def first_step(r, h, here, change):
        pred[r + 1, h] = here + change

    def second_step(r, h, here, change):
        result = 0.5 * (value(r, h) + here + change)
        for t, part in enumerate(columns):
            adv[t, r, h] = result[:, part]

    def guess(r, h):
        return pred[r + 1, h]

    lane = lax.broadcasted_iota(jnp.int32, (8, SLOT), 1)

    def compact(c):
        def body(k, start):
            tile = start >> 7
            shift = start & (SLOT - 1)
            back = (SLOT - shift) & (SLOT - 1)
            take = lane < SLOT - shift
            for i, r in enumerate(chunks[c]):
                parts = []
                for h in range(halves):
                    a = pltpu.roll(adv[tile, r, h], back, axis=1)
                    b = pltpu.roll(adv[tile + 1, r, h], back, axis=1)
                    parts.append(jnp.where(take, a, b))
                send[c, k, :, i * SLOT : (i + 1) * SLOT] = jnp.concatenate(parts, axis=0).astype(BF)
            return start + cnt_ref[0, k]

        lax.fori_loop(0, n_lev, body, jnp.int32(0), unroll=4)

    def ship(c):
        @pl.loop(0, n_lev - 1)
        def _(i):
            peer = peer_of(i)
            pltpu.make_async_remote_copy(
                src_ref=send.at[c, peer],
                dst_ref=recv.at[c, me],
                send_sem=send_sem.at[c],
                recv_sem=recv_sem.at[c],
                device_id={"lev": peer},
                device_id_type=MESH,
            ).start()

        pltpu.make_async_copy(send.at[c, me], recv.at[c, me], recv_sem.at[c]).start()

    adv[tiles] = jnp.zeros(adv.shape[1:], F32)
    for r in range(rows):
        make_side(r)
    for j in range(1, rows):
        make_face(j)
    sweep(value, range(1, 7), first_step)
    sweep(guess, range(2, 6), second_step)
    loads[0].wait()
    compact(0)

    pl.semaphore_wait(barrier, n_lev + 1)

    halos = [
        pltpu.make_async_remote_copy(
            src_ref=src,
            dst_ref=dst,
            send_sem=halo_send.at[i],
            recv_sem=halo_recv.at[i],
            device_id={"lat": other},
            device_id_type=MESH,
        )
        for i, (src, dst, other) in enumerate(((up_buf, lo_buf, up), (down_buf, hi_buf, down)))
    ]
    for halo in halos:
        halo.start()
    ship(0)
    compact(1)
    ship(1)

    for halo in halos:
        halo.wait()
    for r in (-1, rows):
        make_side(r)
    for j in (-1, 0, rows, rows + 1):
        make_face(j)
    sweep(value, (-1, 0), first_step)
    sweep(value, (7, 8), first_step)
    sweep(guess, (0, 1), second_step)
    compact(2)
    ship(2)
    sweep(guess, (6, 7), second_step)
    compact(3)
    ship(3)

    def iota(shape, dim):
        return lax.broadcasted_iota(jnp.int32, shape, dim)

    def hot(mask):
        return jnp.where(mask, 1.0, 0.0).astype(BF)

    def field_of(p):
        return lax.rem(p // levels, fields_count)

    def level_of(p):
        return (p // group) * levels + lax.rem(p, levels)

    def dot(a, b, dims=((1,), (0,))):
        return lax.dot_general(a, b, (dims, ((), ())), preferred_element_type=F32)

    for load in loads[1:]:
        load.wait()
    p_col = iota((feats, feats), 0)
    order = hot(field_of(p_col) * lev_total + level_of(p_col) == iota((feats, feats), 1))
    expand = hot(level_of(iota((feats, lev_total), 0)) == iota((feats, lev_total), 1))
    spread = dot(dot(expand, rw_in[...]).astype(BF), expand, ((1,), (1,)))
    same = field_of(iota((feats, feats), 0)) == field_of(iota((feats, feats), 1))
    mix[...] = jnp.where(same, spread, 0.0).astype(BF)
    w1t[...] = dot(order, w1_in[...]).T.astype(BF)
    w2t[...] = w2_in[...].astype(F32).T.astype(BF)
    w3t[...] = dot(order, w3_in[...].astype(F32).T.astype(BF)).astype(BF)

    def silu(x):
        return x / (1.0 + jnp.exp(-x))

    for c, pair in enumerate(chunks):
        pltpu.make_async_copy(recv.at[c], recv.at[c], recv_sem.at[c]).wait()
        block = recv[c].reshape(feats, 2 * SLOT)
        remapped = block.astype(F32) + dot(mix[...], block)
        hidden = silu(dot(w1t[...], remapped.astype(BF))).astype(BF)
        hidden = silu(dot(w2t[...], hidden)).astype(BF)
        tendency = dot(w3t[...], hidden).astype(BF).astype(F32)
        for i, r in enumerate(pair):
            hit = jnp.max(jnp.where(grp_ref[...] == lat * rows + r, 1.0, 0.0), keepdims=True)
            part = slice(i * SLOT, (i + 1) * SLOT)
            done[pl.ds(r, feats, stride=rows), :] = remapped[:, part] + hit * tendency[:, part]

    keep = lane < cnt_ref[0, me]

    @pl.loop(0, n_lev)
    def _(src):
        for q in range(group):
            tile = done[pl.ds(pl.multiple_of((src * group + q) * rows, rows), rows), :]
            out_ref[q // levels, src * levels + q % levels] = jnp.where(keep, tile, 0.0).astype(BF)

    for c in range(len(chunks)):
        sent = send.at[c, pl.ds(0, n_lev - 1)]
        pltpu.make_async_copy(sent, sent, send_sem.at[c]).wait()


def shards(n_lat, n_lev, x_size, fields, winds, remap_weight, w_first, w_second, w_third, lon_counts, group_list):
    field_count, levels, rows, lon = fields.shape
    group = field_count * levels
    lev_total = remap_weight.shape[0]
    feats = group * n_lev
    hid = w_first.shape[1]
    group_list = group_list.T
    halves = group // 8
    hbm = pl.BlockSpec(memory_space=pltpu.HBM)
    vmem = pl.BlockSpec(memory_space=pltpu.VMEM)
    plane = (8, lon)
    halo = (2 * halves + 2,) + plane
    return pl.pallas_call(
        functools.partial(kernel, n_lat, n_lev, x_size, lev_total),
        out_shape=jax.ShapeDtypeStruct((field_count, lev_total, rows, SLOT), BF),
        in_specs=[hbm, hbm, hbm, hbm, hbm, hbm, hbm, hbm],
        out_specs=vmem,
        scratch_shapes=[
            pltpu.VMEM(halo, F32), pltpu.VMEM(halo, F32),
            pltpu.VMEM(halo, F32), pltpu.VMEM(halo, F32),
            pltpu.VMEM((lon // SLOT, group * rows, SLOT), F32),
            pltpu.VMEM((lon // SLOT, 2 * levels * rows, SLOT), F32),
            pltpu.VMEM((rows, halves) + plane, F32),
            pltpu.VMEM((rows,) + plane, F32), pltpu.VMEM((rows,) + plane, F32),
            pltpu.VMEM((rows + 2,) + plane, F32), pltpu.VMEM((rows + 2,) + plane, F32),
            pltpu.VMEM((rows + 3,) + plane, F32), pltpu.VMEM((rows + 3,) + plane, F32),
            pltpu.VMEM((rows + 2, halves) + plane, F32),
            pltpu.VMEM((lon // SLOT + 1, rows, halves, 8, SLOT), F32),
            pltpu.VMEM((4, n_lev, group, 2 * SLOT), BF),
            pltpu.VMEM((4, n_lev, group, 2 * SLOT), BF),
            pltpu.VMEM(remap_weight.shape, BF), pltpu.VMEM(w_first.shape, BF),
            pltpu.VMEM(w_second.shape, BF), pltpu.VMEM(w_third.shape, BF),
            pltpu.VMEM((feats, feats), BF), pltpu.VMEM((hid, feats), BF),
            pltpu.VMEM((hid, hid), BF), pltpu.VMEM((feats, hid), BF),
            pltpu.VMEM((feats * rows, SLOT), F32),
            pltpu.SemaphoreType.DMA((2,)), pltpu.SemaphoreType.DMA((2,)),
            pltpu.SemaphoreType.DMA((4,)), pltpu.SemaphoreType.DMA((4,)),
            pltpu.SemaphoreType.DMA((6,)), pltpu.SemaphoreType.DMA((2, lon // SLOT)),
            pltpu.SMEM(lon_counts.shape, jnp.int32), pltpu.VMEM(group_list.shape, jnp.int32),
        ],
        compiler_params=pltpu.CompilerParams(
            collective_id=0, has_side_effects=True, vmem_limit_bytes=LIMIT
        ),
    )(*(pltpu.with_memory_space_constraint(x, pltpu.HBM) for x in (
        lon_counts, group_list, fields.reshape(group * rows, lon), winds.reshape(2 * levels * rows, lon),
        remap_weight, w_first, w_second, w_third,
    )))


def solution(mesh):
    n_lat, n_lev = mesh.shape["lat"], mesh.shape["lev"]
    in_specs = (
        P(None, "lev", "lat", None),
        P(None, "lev", "lat", None),
        P(), P(), P(), P(),
        P("lat", None),
        P(),
    )
    return jax.shard_map(
        functools.partial(shards, n_lat, n_lev, 4),
        mesh=mesh,
        in_specs=in_specs,
        out_specs=P(None, None, "lat", "lev"),
        check_vma=False,
    )
```

```python
import functools

import jax
import jax.numpy as jnp
from jax import lax
from jax.experimental import pallas as pl
from jax.experimental.pallas import tpu as pltpu
from jax.sharding import PartitionSpec as P

DIFFUSION = 0.15
SLOT = 128
X_SIZE = 4
LIMIT = 48000000
MESH = pl.DeviceIdType.MESH
BF = jnp.bfloat16
F32 = jnp.float32


def kernel(
    n_lat, n_lev, x_size, lev_total,
    cnt_hbm, grp_hbm, fields_hbm, winds_hbm, rw_hbm, w1_hbm, w2_hbm, w3_hbm,
    out_ref,
    up_buf, down_buf, lo_buf, hi_buf,
    tracer, wind_in, sown, ew, nw, ah, bh, ag, bg, pred,
    raw_out, starts, send, recv,
    rw_in, w1_in, w2_in, w3_in, mix, w1t, w2t, w3t, done,
    halo_send, halo_recv, send_sem, recv_sem, raw_send, raw_recv, load_sem, in_sem, cnt_ref, grp_ref, *raw_in,
):
    rows, fields_count = 8, 4
    group = send.shape[2]
    levels = group // fields_count
    halves = group // 8
    lon = fields_hbm.shape[1]
    feats = n_lev * group
    chunks = ((2, 3), (4, 5), (0, 1), (6, 7))

    lat = lax.axis_index("lat")
    me = lax.axis_index("lev")
    up, down = lax.rem(lat + 1, n_lat), lax.rem(lat + n_lat - 1, n_lat)
    z_size = n_lev // x_size
    my_z, my_x = me // x_size, lax.rem(me, x_size)
    reach = z_size // 2 - 1
    below, above = lax.rem(my_z + z_size - 1, z_size), lax.rem(my_z + 1, z_size)

    def place(z, x):
        return lax.rem(z, z_size) * x_size + lax.rem(x, x_size)

    barrier = pltpu.get_barrier_semaphore()

    def greet(where):
        pl.semaphore_signal(barrier, inc=1, device_id=where, device_id_type=MESH)

    for other in (up, down):
        greet({"lat": other})

    @pl.loop(0, reach * x_size)
    def _(i):
        greet({"lev": place(my_z + 1 + i // x_size, i)})
        greet({"lev": place(my_z + z_size - 1 - i // x_size, i)})

    @pl.loop(1, x_size)
    def _(i):
        greet({"lev": place(my_z, my_x + i)})

    greeted = 2 + 2 * reach * x_size + x_size - 1

    tiles = lon // SLOT
    columns = [slice(t * SLOT, (t + 1) * SLOT) for t in range(tiles)]
    inputs = []
    for t, part in enumerate(columns):
        cut = pl.ds(t * SLOT, SLOT)
        inputs.append(pltpu.make_async_copy(fields_hbm.at[:, cut], tracer.at[t], in_sem.at[0, t]))
        inputs.append(pltpu.make_async_copy(winds_hbm.at[:, cut], wind_in.at[t], in_sem.at[1, t]))
    for copy in inputs:
        copy.start()

    loads = [
        pltpu.make_async_copy(src, dst, load_sem.at[i])
        for i, (src, dst) in enumerate(
            ((cnt_hbm, cnt_ref), (grp_hbm, grp_ref), (rw_hbm, rw_in), (w1_hbm, w1_in), (w2_hbm, w2_in), (w3_hbm, w3_in))
        )
    ]
    for load in loads:
        load.start()

    def twice(x):
        return jnp.concatenate([x, x], axis=0)

    for t, part in enumerate(columns):
        inputs[2 * t].wait()
        inputs[2 * t + 1].wait()
        for r in range(rows):
            for h in range(halves):
                sown[r, h, :, part] = tracer[t, pl.ds(h * 8 * rows + r, 8, stride=rows), :]
            for which, kept in ((0, ew), (1, nw)):
                kept[r, :, part] = twice(wind_in[t, pl.ds(which * levels * rows + r, levels, stride=rows), :])
    for buf, far, near, order in ((up_buf, 6, 7, (6, 7)), (down_buf, 1, 0, (0, 1))):
        for k, r in enumerate(order):
            for h in range(halves):
                buf[k * halves + h] = sown[r, h]
        buf[2 * halves] = jnp.concatenate([ew[near, :levels], nw[near, :levels]], axis=0)
        buf[2 * halves + 1] = nw[far]

    def value(r, h):
        if r < 0:
            return lo_buf[(r + 2) * halves + h]
        if r >= rows:
            return hi_buf[(r - rows) * halves + h]
        return sown[r, h]

    def east(r):
        if r < 0:
            return twice(lo_buf[2 * halves, :levels])
        if r >= rows:
            return twice(hi_buf[2 * halves, :levels])
        return ew[r]

    def north(r):
        if r == -2:
            return lo_buf[2 * halves + 1]
        if r == -1:
            return twice(lo_buf[2 * halves, levels:])
        if r == rows:
            return twice(hi_buf[2 * halves, levels:])
        if r == rows + 1:
            return hi_buf[2 * halves + 1]
        return nw[r]

    def make_side(r):
        u = east(r)
        c = 0.25 * (pltpu.roll(u, 1, axis=1) + u)
        ah[r + 1] = c + DIFFUSION
        bh[r + 1] = c - DIFFUSION

    def make_face(j):
        c = 0.25 * (north(j - 1) + north(j))
        a, b = c + DIFFUSION, c - DIFFUSION
        if j == 0:
            keep = jnp.where(lat > 0, 1.0, 0.0).astype(F32)
            a, b = a * keep, b * keep
        if j == rows:
            keep = jnp.where(lat < n_lat - 1, 1.0, 0.0).astype(F32)
            a, b = a * keep, b * keep
        ag[j + 1] = a
        bg[j + 1] = b

    def sweep(get, span, emit):
        for h in range(halves):
            face = None
            for r in span:
                here = get(r, h)
                if face is None:
                    face = ag[r + 1] * get(r - 1, h) + bg[r + 1] * here
                after = ag[r + 2] * here + bg[r + 2] * get(r + 1, h)
                side = ah[r + 1] * pltpu.roll(here, 1, axis=1) + bh[r + 1] * here
                change = (face - after) + (side - pltpu.roll(side, lon - 1, axis=1))
                emit(r, h, here, change)
                face = after

    def first_step(r, h, here, change):
        pred[r + 1, h] = here + change

    slot_of = {r: (c, i) for c, pair in enumerate(chunks) for i, r in enumerate(pair)}

    def second_step(r, h, here, change):
        c, i = slot_of[r]
        result = (0.5 * (value(r, h) + here + change)).astype(BF)
        for t, part in enumerate(columns):
            raw_out[c, t, i, 8 * h : 8 * h + 8, :] = result[:, part]

    def guess(r, h):
        return pred[r + 1, h]

    lane = lax.broadcasted_iota(jnp.int32, (group, SLOT), 1)
    last_bit = (tiles - 1).bit_length() - 1
    to_right = [reach + 1 if c % 2 == 0 else reach for c in range(len(chunks))]

    def first_slot(c, way):
        return (0, x_size, x_size * (1 + to_right[c]))[way]

    def planes(c, way):
        return (1, to_right[c], 2 * reach + 1 - to_right[c])[way]

    def plane_of(way, j):
        return my_z + z_size - j if way == 2 else my_z + j

    def source_of(way):
        return (me, below * x_size + my_x, above * x_size + my_x)[way]

    def pack(c, way):
        base = first_slot(c, way)

        def body(i, carry):
            start = starts[0, place(plane_of(way, i // x_size), i)]
            tile = start >> 7
            after = (tile + 1) - (tile >> last_bit)
            shift = start & (SLOT - 1)
            back = (SLOT - shift) & (SLOT - 1)
            take = lane < SLOT - shift
            for k in range(2):
                if way == 0:
                    a, b = raw_out[c, tile, k], raw_out[c, after, k]
                else:
                    arrived = raw_in[2 * c + way - 1]
                    a, b = arrived[tile, k], arrived[after, k]
                a, b = pltpu.roll(a, back, axis=1), pltpu.roll(b, back, axis=1)
                send[c, base + i, :, k * SLOT : (k + 1) * SLOT] = jnp.where(take, a, b)
            return carry

        count = planes(c, way) * x_size
        lax.fori_loop(0, count, body, 0, unroll=4 if count % 4 == 0 else 1)

    def slot_copy(c, way, j, x):
        source = source_of(way)
        x = lax.rem(x, x_size)
        return pltpu.make_async_remote_copy(
            src_ref=send.at[c, first_slot(c, way) + j * x_size + x],
            dst_ref=recv.at[c, source],
            send_sem=send_sem.at[c],
            recv_sem=recv_sem.at[c],
            device_id={"lev": place(plane_of(way, j), x)},
            device_id_type=MESH,
        )

    def ship(c, way):
        far = planes(c, way) - 1
        if far > 0:

            @pl.loop(0, far * x_size)
            def _(i):
                slot_copy(c, way, far - i // x_size, i).start()

        @pl.loop(1, x_size)
        def _(i):
            slot_copy(c, way, 0, my_x + i).start()

        mine = send.at[c, first_slot(c, way) + my_x]
        pltpu.make_async_copy(mine, recv.at[c, source_of(way)], recv_sem.at[c]).start()

    def raw_copy(c, w):
        return pltpu.make_async_remote_copy(
            src_ref=raw_out.at[c],
            dst_ref=raw_in[2 * c + w],
            send_sem=raw_send.at[w, c],
            recv_sem=raw_recv.at[w, c],
            device_id={"lev": (above, below)[w] * x_size + my_x},
            device_id_type=MESH,
        )

    def send_raw(c):
        for w in (0, 1):
            raw_copy(c, w).start()

    def relay(c):
        for w in (0, 1):
            raw_copy(c, w).wait_recv()
            pack(c, w + 1)
            ship(c, w + 1)

    def own(c):
        pack(c, 0)
        ship(c, 0)

    for r in range(rows):
        make_side(r)
    for j in range(1, rows):
        make_face(j)
    sweep(value, range(1, 7), first_step)
    sweep(guess, range(2, 6), second_step)
    loads[0].wait()

    def prefix(k, start):
        starts[0, k] = start
        return start + cnt_ref[0, k]

    lax.fori_loop(0, n_lev, prefix, jnp.int32(0))

    pl.semaphore_wait(barrier, greeted)

    halos = [
        pltpu.make_async_remote_copy(
            src_ref=src,
            dst_ref=dst,
            send_sem=halo_send.at[i],
            recv_sem=halo_recv.at[i],
            device_id={"lat": other},
            device_id_type=MESH,
        )
        for i, (src, dst, other) in enumerate(((up_buf, lo_buf, up), (down_buf, hi_buf, down)))
    ]
    for halo in halos:
        halo.start()
    send_raw(0)
    send_raw(1)
    own(0)
    own(1)
    relay(0)

    for halo in halos:
        halo.wait()
    for r in (-1, rows):
        make_side(r)
    for j in (-1, 0, rows, rows + 1):
        make_face(j)
    sweep(value, (-1, 0), first_step)
    sweep(guess, (0, 1), second_step)
    send_raw(2)
    sweep(value, (7, 8), first_step)
    sweep(guess, (6, 7), second_step)
    send_raw(3)
    own(2)
    own(3)
    relay(1)

    def iota(shape, dim):
        return lax.broadcasted_iota(jnp.int32, shape, dim)

    def hot(mask):
        return jnp.where(mask, 1.0, 0.0).astype(BF)

    def field_of(p):
        return lax.rem(p // levels, fields_count)

    def level_of(p):
        return (p // group) * levels + lax.rem(p, levels)

    def dot(a, b, dims=((1,), (0,))):
        return lax.dot_general(a, b, (dims, ((), ())), preferred_element_type=F32)

    for load in loads[1:]:
        load.wait()
    p_col = iota((feats, feats), 0)
    order = hot(field_of(p_col) * lev_total + level_of(p_col) == iota((feats, feats), 1))
    expand = hot(level_of(iota((feats, lev_total), 0)) == iota((feats, lev_total), 1))
    spread = dot(dot(expand, rw_in[...]).astype(BF), expand, ((1,), (1,)))
    same = field_of(iota((feats, feats), 0)) == field_of(iota((feats, feats), 1))
    mix[...] = jnp.where(same, spread, 0.0).astype(BF)
    w1t[...] = dot(order, w1_in[...]).T.astype(BF)
    w2t[...] = w2_in[...].astype(F32).T.astype(BF)
    w3t[...] = dot(order, w3_in[...].astype(F32).T.astype(BF)).astype(BF)

    relay(2)
    relay(3)

    def silu(x):
        return x / (1.0 + jnp.exp(-x))

    for c, pair in enumerate(chunks):
        pltpu.make_async_copy(recv.at[c], recv.at[c], recv_sem.at[c]).wait()
        block = recv[c].reshape(feats, 2 * SLOT)
        remapped = block.astype(F32) + dot(mix[...], block)
        hidden = silu(dot(w1t[...], remapped.astype(BF))).astype(BF)
        hidden = silu(dot(w2t[...], hidden)).astype(BF)
        tendency = dot(w3t[...], hidden).astype(BF).astype(F32)
        for i, r in enumerate(pair):
            hit = jnp.max(jnp.where(grp_ref[...] == lat * rows + r, 1.0, 0.0), keepdims=True)
            part = slice(i * SLOT, (i + 1) * SLOT)
            done[pl.ds(r, feats, stride=rows), :] = remapped[:, part] + hit * tendency[:, part]

    keep = lane[:8] < cnt_ref[0, me]

    @pl.loop(0, n_lev)
    def _(src):
        for q in range(group):
            tile = done[pl.ds(pl.multiple_of((src * group + q) * rows, rows), rows), :]
            out_ref[q // levels, src * levels + q % levels] = jnp.where(keep, tile, 0.0).astype(BF)

    for c in range(len(chunks)):
        sent = send.at[c, pl.ds(0, n_lev - 3)]
        pltpu.make_async_copy(sent, sent, send_sem.at[c]).wait()
        for w in (0, 1):
            raw_copy(c, w).wait_send()


def shards(n_lat, n_lev, x_size, fields, winds, remap_weight, w_first, w_second, w_third, lon_counts, group_list):
    field_count, levels, rows, lon = fields.shape
    group = field_count * levels
    lev_total = remap_weight.shape[0]
    feats = group * n_lev
    hid = w_first.shape[1]
    group_list = group_list.T
    halves = group // 8
    hbm = pl.BlockSpec(memory_space=pltpu.HBM)
    vmem = pl.BlockSpec(memory_space=pltpu.VMEM)
    plane = (8, lon)
    halo = (2 * halves + 2,) + plane
    return pl.pallas_call(
        functools.partial(kernel, n_lat, n_lev, x_size, lev_total),
        out_shape=jax.ShapeDtypeStruct((field_count, lev_total, rows, SLOT), BF),
        in_specs=[hbm, hbm, hbm, hbm, hbm, hbm, hbm, hbm],
        out_specs=vmem,
        scratch_shapes=[
            pltpu.VMEM(halo, F32), pltpu.VMEM(halo, F32),
            pltpu.VMEM(halo, F32), pltpu.VMEM(halo, F32),
            pltpu.VMEM((lon // SLOT, group * rows, SLOT), F32),
            pltpu.VMEM((lon // SLOT, 2 * levels * rows, SLOT), F32),
            pltpu.VMEM((rows, halves) + plane, F32),
            pltpu.VMEM((rows,) + plane, F32), pltpu.VMEM((rows,) + plane, F32),
            pltpu.VMEM((rows + 2,) + plane, F32), pltpu.VMEM((rows + 2,) + plane, F32),
            pltpu.VMEM((rows + 3,) + plane, F32), pltpu.VMEM((rows + 3,) + plane, F32),
            pltpu.VMEM((rows + 2, halves) + plane, F32),
            pltpu.VMEM((4, lon // SLOT, 2, group, SLOT), BF),
            pltpu.SMEM((1, n_lev), jnp.int32),
            pltpu.VMEM((4, n_lev, group, 2 * SLOT), BF),
            pltpu.VMEM((4, n_lev, group, 2 * SLOT), BF),
            pltpu.VMEM(remap_weight.shape, BF), pltpu.VMEM(w_first.shape, BF),
            pltpu.VMEM(w_second.shape, BF), pltpu.VMEM(w_third.shape, BF),
            pltpu.VMEM((feats, feats), BF), pltpu.VMEM((hid, feats), BF),
            pltpu.VMEM((hid, hid), BF), pltpu.VMEM((feats, hid), BF),
            pltpu.VMEM((feats * rows, SLOT), F32),
            pltpu.SemaphoreType.DMA((2,)), pltpu.SemaphoreType.DMA((2,)),
            pltpu.SemaphoreType.DMA((4,)), pltpu.SemaphoreType.DMA((4,)),
            pltpu.SemaphoreType.DMA((2, 4)), pltpu.SemaphoreType.DMA((2, 4)),
            pltpu.SemaphoreType.DMA((6,)), pltpu.SemaphoreType.DMA((2, lon // SLOT)),
            pltpu.SMEM(lon_counts.shape, jnp.int32), pltpu.VMEM(group_list.shape, jnp.int32),
            *[pltpu.VMEM((lon // SLOT, 2, group, SLOT), BF)] * 8,
        ],
        compiler_params=pltpu.CompilerParams(
            collective_id=0, has_side_effects=True, vmem_limit_bytes=LIMIT
        ),
    )(*(pltpu.with_memory_space_constraint(x, pltpu.HBM) for x in (
        lon_counts, group_list, fields.reshape(group * rows, lon), winds.reshape(2 * levels * rows, lon),
        remap_weight, w_first, w_second, w_third,
    )))


def solution(mesh):
    n_lat, n_lev = mesh.shape["lat"], mesh.shape["lev"]
    in_specs = (
        P(None, "lev", "lat", None),
        P(None, "lev", "lat", None),
        P(), P(), P(), P(),
        P("lat", None),
        P(),
    )
    return jax.shard_map(
        functools.partial(shards, n_lat, n_lev, X_SIZE),
        mesh=mesh,
        in_specs=in_specs,
        out_specs=P(None, None, "lat", "lev"),
        check_vma=False,
    )
```

```python
import functools

import jax
import jax.numpy as jnp
from jax import lax
from jax.experimental import pallas as pl
from jax.experimental.pallas import tpu as pltpu
from jax.sharding import PartitionSpec as P

DIFFUSION = 0.15
SLOT = 128
X_SIZE = 4
LIMIT = 48000000
MESH = pl.DeviceIdType.MESH
BF = jnp.bfloat16
F32 = jnp.float32


def kernel(
    n_lat, n_lev, x_size, lev_total,
    cnt_hbm, grp_hbm, fields_hbm, winds_hbm, rw_hbm, w1_hbm, w2_hbm, w3_hbm,
    out_ref,
    up_buf, down_buf, lo_buf, hi_buf,
    tracer, wind_in, sown, ew, nw, ah, bh, ag, bg, pred,
    raw_out, starts, send, recv,
    rw_in, w1_in, w2_in, w3_in, mix, w1t, w2t, w3t, done,
    halo_send, halo_recv, send_sem, recv_sem, raw_send, raw_recv, fwd_send, fwd_recv, load_sem, in_sem, cnt_ref, grp_ref, *raw_bufs,
):
    rows, fields_count = 8, 4
    group = send.shape[2]
    levels = group // fields_count
    halves = group // 8
    lon = fields_hbm.shape[1]
    feats = n_lev * group
    chunks = ((2, 3), (4, 5), (0, 1), (6, 7))

    lat = lax.axis_index("lat")
    me = lax.axis_index("lev")
    up, down = lax.rem(lat + 1, n_lat), lax.rem(lat + n_lat - 1, n_lat)
    z_size = n_lev // x_size
    my_z, my_x = me // x_size, lax.rem(me, x_size)
    reach = z_size // 2 - 1
    below, above = lax.rem(my_z + z_size - 1, z_size), lax.rem(my_z + 1, z_size)

    def place(z, x):
        return lax.rem(z, z_size) * x_size + lax.rem(x, x_size)

    tiles = lon // SLOT
    columns = [slice(t * SLOT, (t + 1) * SLOT) for t in range(tiles)]
    inputs = []
    for t, part in enumerate(columns):
        cut = pl.ds(t * SLOT, SLOT)
        inputs.append(pltpu.make_async_copy(fields_hbm.at[:, cut], tracer.at[t], in_sem.at[0, t]))
        inputs.append(pltpu.make_async_copy(winds_hbm.at[:, cut], wind_in.at[t], in_sem.at[1, t]))
    for copy in inputs:
        copy.start()

    barrier = pltpu.get_barrier_semaphore()

    def greet(where):
        pl.semaphore_signal(barrier, inc=1, device_id=where, device_id_type=MESH)

    for other in (up, down):
        greet({"lat": other})

    near = max(1, reach - 1)

    @pl.loop(0, near * x_size)
    def _(i):
        greet({"lev": place(my_z + 1 + i // x_size, i)})
        greet({"lev": place(my_z + z_size - 1 - i // x_size, i)})

    @pl.loop(1, x_size)
    def _(i):
        greet({"lev": place(my_z, my_x + i)})

    greeted = 2 + 2 * near * x_size + x_size - 1

    loads = [
        pltpu.make_async_copy(src, dst, load_sem.at[i])
        for i, (src, dst) in enumerate(
            ((cnt_hbm, cnt_ref), (grp_hbm, grp_ref), (rw_hbm, rw_in), (w1_hbm, w1_in), (w2_hbm, w2_in), (w3_hbm, w3_in))
        )
    ]
    for load in loads:
        load.start()

    def twice(x):
        return jnp.concatenate([x, x], axis=0)

    for t, part in enumerate(columns):
        inputs[2 * t].wait()
        inputs[2 * t + 1].wait()
        for r in range(rows):
            for h in range(halves):
                sown[r, h, :, part] = tracer[t, pl.ds(h * 8 * rows + r, 8, stride=rows), :]
            for which, kept in ((0, ew), (1, nw)):
                kept[r, :, part] = twice(wind_in[t, pl.ds(which * levels * rows + r, levels, stride=rows), :])
    for buf, far, near, order in ((up_buf, 6, 7, (6, 7)), (down_buf, 1, 0, (0, 1))):
        for k, r in enumerate(order):
            for h in range(halves):
                buf[k * halves + h] = sown[r, h]
        buf[2 * halves] = jnp.concatenate([ew[near, :levels], nw[near, :levels]], axis=0)
        buf[2 * halves + 1] = nw[far]

    def value(r, h):
        if r < 0:
            return lo_buf[(r + 2) * halves + h]
        if r >= rows:
            return hi_buf[(r - rows) * halves + h]
        return sown[r, h]

    def east(r):
        if r < 0:
            return twice(lo_buf[2 * halves, :levels])
        if r >= rows:
            return twice(hi_buf[2 * halves, :levels])
        return ew[r]

    def north(r):
        if r == -2:
            return lo_buf[2 * halves + 1]
        if r == -1:
            return twice(lo_buf[2 * halves, levels:])
        if r == rows:
            return twice(hi_buf[2 * halves, levels:])
        if r == rows + 1:
            return hi_buf[2 * halves + 1]
        return nw[r]

    def make_side(r):
        u = east(r)
        c = 0.25 * (pltpu.roll(u, 1, axis=1) + u)
        ah[r + 1] = c + DIFFUSION
        bh[r + 1] = c - DIFFUSION

    def make_face(j):
        c = 0.25 * (north(j - 1) + north(j))
        a, b = c + DIFFUSION, c - DIFFUSION
        if j == 0:
            keep = jnp.where(lat > 0, 1.0, 0.0).astype(F32)
            a, b = a * keep, b * keep
        if j == rows:
            keep = jnp.where(lat < n_lat - 1, 1.0, 0.0).astype(F32)
            a, b = a * keep, b * keep
        ag[j + 1] = a
        bg[j + 1] = b

    def sweep(get, span, emit):
        for h in range(halves):
            face = None
            for r in span:
                here = get(r, h)
                if face is None:
                    face = ag[r + 1] * get(r - 1, h) + bg[r + 1] * here
                after = ag[r + 2] * here + bg[r + 2] * get(r + 1, h)
                side = ah[r + 1] * pltpu.roll(here, 1, axis=1) + bh[r + 1] * here
                change = (face - after) + (side - pltpu.roll(side, lon - 1, axis=1))
                emit(r, h, here, change)
                face = after

    def first_step(r, h, here, change):
        pred[r + 1, h] = here + change

    slot_of = {r: (c, i) for c, pair in enumerate(chunks) for i, r in enumerate(pair)}

    def second_step(r, h, here, change):
        c, i = slot_of[r]
        result = (0.5 * (value(r, h) + here + change)).astype(BF)
        for t, part in enumerate(columns):
            raw_out[c, t, i, 8 * h : 8 * h + 8, :] = result[:, part]

    def guess(r, h):
        return pred[r + 1, h]

    lane = lax.broadcasted_iota(jnp.int32, (group, SLOT), 1)
    last_bit = (tiles - 1).bit_length() - 1
    raw_in, raw_far = raw_bufs[:8], raw_bufs[8:]

    def part_of(c, k):
        side = c % 2
        ups = (1 - 2 * side) % z_size
        nears = [below * x_size + my_x, above * x_size + my_x]
        if k == 0:
            return 0, 1, 1, me, raw_out.at[c]
        if k == 1:
            return x_size, 1, 1, nears[side], raw_in[2 * c + side]
        if k == 2:
            return 2 * x_size, reach, ups, place(my_z + (z_size - 2, 2)[side], 0) + my_x, raw_far[c]
        return (2 + reach) * x_size, reach, z_size - ups, nears[1 - side], raw_in[2 * c + 1 - side]

    def pack(c, k):
        base, count, step, _, rows_in = part_of(c, k)

        def body(i, carry):
            start = starts[0, place(my_z + (i // x_size) * step, i)]
            tile = start >> 7
            after = (tile + 1) - (tile >> last_bit)
            shift = start & (SLOT - 1)
            back = (SLOT - shift) & (SLOT - 1)
            take = lane < SLOT - shift
            for q in range(2):
                a = pltpu.roll(rows_in[tile, q], back, axis=1)
                b = pltpu.roll(rows_in[after, q], back, axis=1)
                send[c, base + i, :, q * SLOT : (q + 1) * SLOT] = jnp.where(take, a, b)
            return carry

        lax.fori_loop(0, count * x_size, body, 0, unroll=4 if x_size == 4 else 1)

    def slot_copy(c, k, j, x):
        base, _, step, source, _ = part_of(c, k)
        x = lax.rem(x, x_size)
        return pltpu.make_async_remote_copy(
            src_ref=send.at[c, base + j * x_size + x],
            dst_ref=recv.at[c, source],
            send_sem=send_sem.at[c],
            recv_sem=recv_sem.at[c],
            device_id={"lev": place(my_z + j * step, x)},
            device_id_type=MESH,
        )

    def ship(c, k):
        base, count, _, source, _ = part_of(c, k)
        if count > 1:

            @pl.loop(0, (count - 1) * x_size)
            def _(i):
                slot_copy(c, k, count - 1 - i // x_size, i).start()

        @pl.loop(1, x_size)
        def _(i):
            slot_copy(c, k, 0, my_x + i).start()

        pltpu.make_async_copy(send.at[c, base + my_x], recv.at[c, source], recv_sem.at[c]).start()

    def raw_copy(c, w):
        return pltpu.make_async_remote_copy(
            src_ref=raw_out.at[c],
            dst_ref=raw_in[2 * c + w],
            send_sem=raw_send.at[w, c],
            recv_sem=raw_recv.at[w, c],
            device_id={"lev": (above, below)[w] * x_size + my_x},
            device_id_type=MESH,
        )

    def forward_copy(c):
        side = c % 2
        return pltpu.make_async_remote_copy(
            src_ref=raw_in[2 * c + side],
            dst_ref=raw_far[c],
            send_sem=fwd_send.at[c],
            recv_sem=fwd_recv.at[c],
            device_id={"lev": (above, below)[side] * x_size + my_x},
            device_id_type=MESH,
        )

    def send_raw(c):
        for w in (0, 1):
            raw_copy(c, w).start()

    def relay(c):
        side = c % 2
        raw_copy(c, side).wait_recv()
        forward_copy(c).start()
        pack(c, 1)
        ship(c, 1)
        raw_copy(c, 1 - side).wait_recv()
        pack(c, 3)
        ship(c, 3)

    def relay_far(c):
        forward_copy(c).wait_recv()
        pack(c, 2)
        ship(c, 2)

    def own(c):
        pack(c, 0)
        ship(c, 0)

    for r in range(1, 5):
        make_side(r)
    for j in range(1, 6):
        make_face(j)
    sweep(value, range(1, 5), first_step)
    sweep(guess, (2, 3), second_step)

    pl.semaphore_wait(barrier, greeted)

    halos = [
        pltpu.make_async_remote_copy(
            src_ref=src,
            dst_ref=dst,
            send_sem=halo_send.at[i],
            recv_sem=halo_recv.at[i],
            device_id={"lat": other},
            device_id_type=MESH,
        )
        for i, (src, dst, other) in enumerate(((up_buf, lo_buf, up), (down_buf, hi_buf, down)))
    ]
    for halo in halos:
        halo.start()
    send_raw(0)
    for r in (5, 6):
        make_side(r)
    for j in (6, 7):
        make_face(j)
    sweep(value, (5, 6), first_step)
    sweep(guess, (4, 5), second_step)
    send_raw(1)
    for r in (0, 7):
        make_side(r)
    loads[0].wait()

    def prefix(k, start):
        starts[0, k] = start
        return start + cnt_ref[0, k]

    lax.fori_loop(0, n_lev, prefix, jnp.int32(0))
    own(0)
    own(1)
    relay(0)

    for halo in halos:
        halo.wait()
    for r in (-1, rows):
        make_side(r)
    for j in (-1, 0, rows, rows + 1):
        make_face(j)
    sweep(value, (-1, 0), first_step)
    sweep(guess, (0, 1), second_step)
    send_raw(2)
    sweep(value, (7, 8), first_step)
    sweep(guess, (6, 7), second_step)
    send_raw(3)
    own(2)
    own(3)
    relay(1)
    relay_far(0)
    relay_far(1)

    def iota(shape, dim):
        return lax.broadcasted_iota(jnp.int32, shape, dim)

    def hot(mask):
        return jnp.where(mask, 1.0, 0.0).astype(BF)

    def field_of(p):
        return lax.rem(p // levels, fields_count)

    def level_of(p):
        return (p // group) * levels + lax.rem(p, levels)

    def dot(a, b, dims=((1,), (0,))):
        return lax.dot_general(a, b, (dims, ((), ())), preferred_element_type=F32)

    for load in loads[1:]:
        load.wait()
    p_col = iota((feats, feats), 0)
    order = hot(field_of(p_col) * lev_total + level_of(p_col) == iota((feats, feats), 1))
    expand = hot(level_of(iota((feats, lev_total), 0)) == iota((feats, lev_total), 1))
    spread = dot(dot(expand, rw_in[...]).astype(BF), expand, ((1,), (1,)))
    same = field_of(iota((feats, feats), 0)) == field_of(iota((feats, feats), 1))
    mix[...] = jnp.where(same, spread, 0.0).astype(BF)
    w1t[...] = dot(order, w1_in[...]).T.astype(BF)
    w2t[...] = w2_in[...].astype(F32).T.astype(BF)
    w3t[...] = dot(order, w3_in[...].astype(F32).T.astype(BF)).astype(BF)

    relay(2)
    relay(3)
    relay_far(2)
    relay_far(3)

    def silu(x):
        return x / (1.0 + jnp.exp(-x))

    for c, pair in enumerate(chunks):
        pltpu.make_async_copy(recv.at[c], recv.at[c], recv_sem.at[c]).wait()
        block = recv[c].reshape(feats, 2 * SLOT)
        remapped = block.astype(F32) + dot(mix[...], block)
        hidden = silu(dot(w1t[...], remapped.astype(BF))).astype(BF)
        hidden = silu(dot(w2t[...], hidden)).astype(BF)
        tendency = dot(w3t[...], hidden).astype(BF).astype(F32)
        for i, r in enumerate(pair):
            hit = jnp.max(jnp.where(grp_ref[...] == lat * rows + r, 1.0, 0.0), keepdims=True)
            part = slice(i * SLOT, (i + 1) * SLOT)
            done[pl.ds(r, feats, stride=rows), :] = remapped[:, part] + hit * tendency[:, part]

    keep = lane[:8] < cnt_ref[0, me]

    @pl.loop(0, n_lev)
    def _(src):
        for q in range(group):
            tile = done[pl.ds(pl.multiple_of((src * group + q) * rows, rows), rows), :]
            out_ref[q // levels, src * levels + q % levels] = jnp.where(keep, tile, 0.0).astype(BF)

    for c in range(len(chunks)):
        sent = send.at[c, pl.ds(0, n_lev - 4)]
        pltpu.make_async_copy(sent, sent, send_sem.at[c]).wait()
        for w in (0, 1):
            raw_copy(c, w).wait_send()
        forward_copy(c).wait_send()


def shards(n_lat, n_lev, x_size, fields, winds, remap_weight, w_first, w_second, w_third, lon_counts, group_list):
    field_count, levels, rows, lon = fields.shape
    group = field_count * levels
    lev_total = remap_weight.shape[0]
    feats = group * n_lev
    hid = w_first.shape[1]
    group_list = group_list.T
    halves = group // 8
    hbm = pl.BlockSpec(memory_space=pltpu.HBM)
    vmem = pl.BlockSpec(memory_space=pltpu.VMEM)
    plane = (8, lon)
    halo = (2 * halves + 2,) + plane
    return pl.pallas_call(
        functools.partial(kernel, n_lat, n_lev, x_size, lev_total),
        out_shape=jax.ShapeDtypeStruct((field_count, lev_total, rows, SLOT), BF),
        in_specs=[hbm, hbm, hbm, hbm, hbm, hbm, hbm, hbm],
        out_specs=vmem,
        scratch_shapes=[
            pltpu.VMEM(halo, F32), pltpu.VMEM(halo, F32),
            pltpu.VMEM(halo, F32), pltpu.VMEM(halo, F32),
            pltpu.VMEM((lon // SLOT, group * rows, SLOT), F32),
            pltpu.VMEM((lon // SLOT, 2 * levels * rows, SLOT), F32),
            pltpu.VMEM((rows, halves) + plane, F32),
            pltpu.VMEM((rows,) + plane, F32), pltpu.VMEM((rows,) + plane, F32),
            pltpu.VMEM((rows + 2,) + plane, F32), pltpu.VMEM((rows + 2,) + plane, F32),
            pltpu.VMEM((rows + 3,) + plane, F32), pltpu.VMEM((rows + 3,) + plane, F32),
            pltpu.VMEM((rows + 2, halves) + plane, F32),
            pltpu.VMEM((4, lon // SLOT, 2, group, SLOT), BF),
            pltpu.SMEM((1, n_lev), jnp.int32),
            pltpu.VMEM((4, n_lev, group, 2 * SLOT), BF),
            pltpu.VMEM((4, n_lev, group, 2 * SLOT), BF),
            pltpu.VMEM(remap_weight.shape, BF), pltpu.VMEM(w_first.shape, BF),
            pltpu.VMEM(w_second.shape, BF), pltpu.VMEM(w_third.shape, BF),
            pltpu.VMEM((feats, feats), BF), pltpu.VMEM((hid, feats), BF),
            pltpu.VMEM((hid, hid), BF), pltpu.VMEM((feats, hid), BF),
            pltpu.VMEM((feats * rows, SLOT), F32),
            pltpu.SemaphoreType.DMA((2,)), pltpu.SemaphoreType.DMA((2,)),
            pltpu.SemaphoreType.DMA((4,)), pltpu.SemaphoreType.DMA((4,)),
            pltpu.SemaphoreType.DMA((2, 4)), pltpu.SemaphoreType.DMA((2, 4)),
            pltpu.SemaphoreType.DMA((4,)), pltpu.SemaphoreType.DMA((4,)),
            pltpu.SemaphoreType.DMA((6,)), pltpu.SemaphoreType.DMA((2, lon // SLOT)),
            pltpu.SMEM(lon_counts.shape, jnp.int32), pltpu.VMEM(group_list.shape, jnp.int32),
            *[pltpu.VMEM((lon // SLOT, 2, group, SLOT), BF)] * 12,
        ],
        compiler_params=pltpu.CompilerParams(
            collective_id=0, has_side_effects=True, vmem_limit_bytes=LIMIT
        ),
    )(*(pltpu.with_memory_space_constraint(x, pltpu.HBM) for x in (
        lon_counts, group_list, fields.reshape(group * rows, lon), winds.reshape(2 * levels * rows, lon),
        remap_weight, w_first, w_second, w_third,
    )))


def solution(mesh):
    n_lat, n_lev = mesh.shape["lat"], mesh.shape["lev"]
    in_specs = (
        P(None, "lev", "lat", None),
        P(None, "lev", "lat", None),
        P(), P(), P(), P(),
        P("lat", None),
        P(),
    )
    return jax.shard_map(
        functools.partial(shards, n_lat, n_lev, X_SIZE),
        mesh=mesh,
        in_specs=in_specs,
        out_specs=P(None, None, "lat", "lev"),
        check_vma=False,
    )
```

```python
import functools

import jax
import jax.numpy as jnp
from jax import lax
from jax.experimental import pallas as pl
from jax.experimental.pallas import tpu as pltpu
from jax.sharding import PartitionSpec as P

DIFFUSION = 0.15
SLOT = 128
X_SIZE = 4
LIMIT = 48000000
MESH = pl.DeviceIdType.MESH
BF = jnp.bfloat16
F32 = jnp.float32


def kernel(
    n_lat, n_lev, x_size, lev_total,
    cnt_hbm, grp_hbm, fields_hbm, winds_hbm, rw_hbm, w1_hbm, w2_hbm, w3_hbm,
    out_ref,
    up_buf, down_buf, lo_buf, hi_buf,
    tracer, wind_in, sown, ew, nw, ah, bh, ag, bg, pred,
    raw_out, starts, send, recv,
    rw_in, w1_in, w2_in, w3_in, mix, w1t, w2t, w3t, done,
    halo_send, halo_recv, send_sem, recv_sem, raw_send, raw_recv, load_sem, in_sem, cnt_ref, grp_ref, *raw_in,
):
    rows, fields_count = 8, 4
    group = send.shape[2]
    levels = group // fields_count
    halves = group // 8
    lon = fields_hbm.shape[1]
    feats = n_lev * group
    chunks = ((2, 3), (4, 5), (0, 1), (6, 7))

    lat = lax.axis_index("lat")
    me = lax.axis_index("lev")
    up, down = lax.rem(lat + 1, n_lat), lax.rem(lat + n_lat - 1, n_lat)
    z_size = n_lev // x_size
    my_z, my_x = me // x_size, lax.rem(me, x_size)
    reach = z_size // 2 - 1
    plane_at = {d: lax.rem(my_z + z_size + d, z_size) * x_size for d in range(-reach, reach + 1)}
    x_at = [lax.rem(my_x + i, x_size) for i in range(x_size)]

    tiles = lon // SLOT
    columns = [slice(t * SLOT, (t + 1) * SLOT) for t in range(tiles)]
    inputs = []
    for t, part in enumerate(columns):
        cut = pl.ds(t * SLOT, SLOT)
        inputs.append(pltpu.make_async_copy(fields_hbm.at[:, cut], tracer.at[t], in_sem.at[0, t]))
        inputs.append(pltpu.make_async_copy(winds_hbm.at[:, cut], wind_in.at[t], in_sem.at[1, t]))
    for copy in inputs:
        copy.start()

    barrier = pltpu.get_barrier_semaphore()

    def greet(where):
        pl.semaphore_signal(barrier, inc=1, device_id=where, device_id_type=MESH)

    for other in (up, down):
        greet({"lat": other})

    for d in range(1, reach + 1):

        @pl.loop(0, x_size)
        def _(x, d=d):
            greet({"lev": plane_at[d] + x})
            greet({"lev": plane_at[-d] + x})

    for x in x_at[1:]:
        greet({"lev": plane_at[0] + x})

    greeted = 2 + 2 * reach * x_size + x_size - 1

    loads = [
        pltpu.make_async_copy(src, dst, load_sem.at[i])
        for i, (src, dst) in enumerate(
            ((cnt_hbm, cnt_ref), (grp_hbm, grp_ref), (rw_hbm, rw_in), (w1_hbm, w1_in), (w2_hbm, w2_in), (w3_hbm, w3_in))
        )
    ]
    for load in loads:
        load.start()

    def twice(x):
        return jnp.concatenate([x, x], axis=0)

    for t, part in enumerate(columns):
        inputs[2 * t].wait()
        inputs[2 * t + 1].wait()
        for r in range(rows):
            for h in range(halves):
                sown[r, h, :, part] = tracer[t, pl.ds(h * 8 * rows + r, 8, stride=rows), :]
            for which, kept in ((0, ew), (1, nw)):
                kept[r, :, part] = twice(wind_in[t, pl.ds(which * levels * rows + r, levels, stride=rows), :])
    for buf, far, near, order in ((up_buf, 6, 7, (6, 7)), (down_buf, 1, 0, (0, 1))):
        for k, r in enumerate(order):
            for h in range(halves):
                buf[k * halves + h] = sown[r, h]
        buf[2 * halves] = jnp.concatenate([ew[near, :levels], nw[near, :levels]], axis=0)
        buf[2 * halves + 1] = nw[far]

    def value(r, h):
        if r < 0:
            return lo_buf[(r + 2) * halves + h]
        if r >= rows:
            return hi_buf[(r - rows) * halves + h]
        return sown[r, h]

    def east(r):
        if r < 0:
            return twice(lo_buf[2 * halves, :levels])
        if r >= rows:
            return twice(hi_buf[2 * halves, :levels])
        return ew[r]

    def north(r):
        if r == -2:
            return lo_buf[2 * halves + 1]
        if r == -1:
            return twice(lo_buf[2 * halves, levels:])
        if r == rows:
            return twice(hi_buf[2 * halves, levels:])
        if r == rows + 1:
            return hi_buf[2 * halves + 1]
        return nw[r]

    def make_side(r):
        u = east(r)
        c = 0.25 * (pltpu.roll(u, 1, axis=1) + u)
        ah[r + 1] = c + DIFFUSION
        bh[r + 1] = c - DIFFUSION

    def make_face(j):
        c = 0.25 * (north(j - 1) + north(j))
        a, b = c + DIFFUSION, c - DIFFUSION
        if j == 0:
            keep = jnp.where(lat > 0, 1.0, 0.0).astype(F32)
            a, b = a * keep, b * keep
        if j == rows:
            keep = jnp.where(lat < n_lat - 1, 1.0, 0.0).astype(F32)
            a, b = a * keep, b * keep
        ag[j + 1] = a
        bg[j + 1] = b

    def sweep(get, span, emit):
        for h in range(halves):
            face = None
            for r in span:
                here = get(r, h)
                if face is None:
                    face = ag[r + 1] * get(r - 1, h) + bg[r + 1] * here
                after = ag[r + 2] * here + bg[r + 2] * get(r + 1, h)
                side = ah[r + 1] * pltpu.roll(here, 1, axis=1) + bh[r + 1] * here
                change = (face - after) + (side - pltpu.roll(side, lon - 1, axis=1))
                emit(r, h, here, change)
                face = after

    def first_step(r, h, here, change):
        pred[r + 1, h] = here + change

    slot_of = {r: (c, i) for c, pair in enumerate(chunks) for i, r in enumerate(pair)}

    def second_step(r, h, here, change):
        c, i = slot_of[r]
        result = (0.5 * (value(r, h) + here + change)).astype(BF)
        for t, part in enumerate(columns):
            raw_out[c, t, i, 8 * h : 8 * h + 8, :] = result[:, part]

    def guess(r, h):
        return pred[r + 1, h]

    lane = lax.broadcasted_iota(jnp.int32, (group, SLOT), 1)
    last_bit = (tiles - 1).bit_length() - 1
    half = x_size // 2

    def first_slot(way):
        return (0, x_size, x_size * (1 + reach) + half)[way]

    def planes(way):
        return (1, reach + 1, reach + 1)[way]

    def chips(way, j):
        if j < reach:
            return range(x_size)
        return range(half) if way == 1 else range(half, x_size)

    def slot(way, j, x):
        return first_slot(way) + j * x_size + x - (half if way == 2 and j == reach else 0)

    def plane_of(way, j):
        return plane_at[-j if way == 2 else j]

    def source_of(way):
        return plane_at[(0, -1, 1)[way]] + my_x

    def pack(c, way):
        for j in range(planes(way)):
            owners = plane_of(way, j)
            for x in chips(way, j):
                start = starts[0, owners + x]
                tile = start >> 7
                after = (tile + 1) - (tile >> last_bit)
                shift = start & (SLOT - 1)
                back = (SLOT - shift) & (SLOT - 1)
                take = lane < SLOT - shift
                for k in range(2):
                    if way == 0:
                        a, b = raw_out[c, tile, k], raw_out[c, after, k]
                    else:
                        arrived = raw_in[2 * c + way - 1]
                        a, b = arrived[tile, k], arrived[after, k]
                    a, b = pltpu.roll(a, back, axis=1), pltpu.roll(b, back, axis=1)
                    send[c, slot(way, j, x), :, k * SLOT : (k + 1) * SLOT] = jnp.where(take, a, b)

    def slot_copy(c, way, j, x):
        return pltpu.make_async_remote_copy(
            src_ref=send.at[c, slot(way, j, x)],
            dst_ref=recv.at[c, source_of(way)],
            send_sem=send_sem.at[c],
            recv_sem=recv_sem.at[c],
            device_id={"lev": plane_of(way, j) + x},
            device_id_type=MESH,
        )

    def ship(c, way):
        for j in range(planes(way) - 1, 0, -1):
            span = chips(way, j)

            @pl.loop(span[0], span[-1] + 1)
            def _(x, j=j):
                slot_copy(c, way, j, x).start()

        for x in x_at[1:]:
            slot_copy(c, way, 0, x).start()

        mine = send.at[c, first_slot(way) + my_x]
        pltpu.make_async_copy(mine, recv.at[c, source_of(way)], recv_sem.at[c]).start()

    def raw_copy(c, w):
        return pltpu.make_async_remote_copy(
            src_ref=raw_out.at[c],
            dst_ref=raw_in[2 * c + w],
            send_sem=raw_send.at[w, c],
            recv_sem=raw_recv.at[w, c],
            device_id={"lev": plane_at[(1, -1)[w]] + my_x},
            device_id_type=MESH,
        )

    def send_raw(c):
        for w in (0, 1):
            raw_copy(c, w).start()

    def relay(c):
        for w in (0, 1):
            raw_copy(c, w).wait_recv()
            pack(c, w + 1)
            ship(c, w + 1)

    def own(c):
        pack(c, 0)
        ship(c, 0)

    for r in range(1, 5):
        make_side(r)
    for j in range(1, 6):
        make_face(j)
    sweep(value, range(1, 5), first_step)
    sweep(guess, (2, 3), second_step)

    pl.semaphore_wait(barrier, greeted)

    halos = [
        pltpu.make_async_remote_copy(
            src_ref=src,
            dst_ref=dst,
            send_sem=halo_send.at[i],
            recv_sem=halo_recv.at[i],
            device_id={"lat": other},
            device_id_type=MESH,
        )
        for i, (src, dst, other) in enumerate(((up_buf, lo_buf, up), (down_buf, hi_buf, down)))
    ]
    for halo in halos:
        halo.start()
    send_raw(0)
    for r in (5, 6):
        make_side(r)
    for j in (6, 7):
        make_face(j)
    sweep(value, (5, 6), first_step)
    sweep(guess, (4, 5), second_step)
    send_raw(1)
    for r in (0, 7):
        make_side(r)
    loads[0].wait()

    def prefix(k, start):
        starts[0, k] = start
        return start + cnt_ref[0, k]

    lax.fori_loop(0, n_lev, prefix, jnp.int32(0))
    own(0)
    own(1)
    relay(0)

    for halo in halos:
        halo.wait()
    for r in (-1, rows):
        make_side(r)
    for j in (-1, 0, rows, rows + 1):
        make_face(j)
    sweep(value, (-1, 0), first_step)
    sweep(guess, (0, 1), second_step)
    send_raw(2)
    sweep(value, (7, 8), first_step)
    sweep(guess, (6, 7), second_step)
    send_raw(3)
    own(2)
    own(3)
    relay(1)

    relay(2)
    relay(3)

    def iota(shape, dim):
        return lax.broadcasted_iota(jnp.int32, shape, dim)

    def hot(mask):
        return jnp.where(mask, 1.0, 0.0).astype(BF)

    def field_of(p):
        return lax.rem(p // levels, fields_count)

    def level_of(p):
        return (p // group) * levels + lax.rem(p, levels)

    def dot(a, b, dims=((1,), (0,))):
        return lax.dot_general(a, b, (dims, ((), ())), preferred_element_type=F32)

    for load in loads[1:]:
        load.wait()
    p_col = iota((feats, feats), 0)
    order = hot(field_of(p_col) * lev_total + level_of(p_col) == iota((feats, feats), 1))
    expand = hot(level_of(iota((feats, lev_total), 0)) == iota((feats, lev_total), 1))
    spread = dot(dot(expand, rw_in[...]).astype(BF), expand, ((1,), (1,)))
    same = field_of(iota((feats, feats), 0)) == field_of(iota((feats, feats), 1))
    mix[...] = jnp.where(same, spread, 0.0).astype(BF)
    w1t[...] = dot(order, w1_in[...]).T.astype(BF)
    w2t[...] = w2_in[...].astype(F32).T.astype(BF)
    w3t[...] = dot(order, w3_in[...].astype(F32).T.astype(BF)).astype(BF)

    def silu(x):
        half = 0.5 * x
        return half + half * jnp.tanh(half)

    for c, pair in enumerate(chunks):
        pltpu.make_async_copy(recv.at[c], recv.at[c], recv_sem.at[c]).wait()
        block = recv[c].reshape(feats, 2 * SLOT)
        remapped = block.astype(F32) + dot(mix[...], block)
        hidden = silu(dot(w1t[...], remapped.astype(BF))).astype(BF)
        hidden = silu(dot(w2t[...], hidden)).astype(BF)
        tendency = dot(w3t[...], hidden).astype(BF).astype(F32)
        for i, r in enumerate(pair):
            hit = jnp.max(jnp.where(grp_ref[...] == lat * rows + r, 1.0, 0.0), keepdims=True)
            part = slice(i * SLOT, (i + 1) * SLOT)
            done[pl.ds(r, feats, stride=rows), :] = remapped[:, part] + hit * tendency[:, part]

    span = levels * rows
    keep = lax.broadcasted_iota(jnp.int32, (span, SLOT), 1) < cnt_ref[0, me]

    def finish(src, carry):
        for f in range(fields_count):
            part = done[pl.ds(pl.multiple_of((src * fields_count + f) * span, span), span), :]
            where = pl.multiple_of((f * n_lev + src) * span, span)
            out_ref[pl.ds(where, span), :] = jnp.where(keep, part, 0.0).astype(BF)
        return carry

    lax.fori_loop(0, n_lev, finish, 0, unroll=4)

    for c in range(len(chunks)):
        sent = send.at[c, pl.ds(0, n_lev - 3)]
        pltpu.make_async_copy(sent, sent, send_sem.at[c]).wait()
        for w in (0, 1):
            raw_copy(c, w).wait_send()


def shards(n_lat, n_lev, x_size, fields, winds, remap_weight, w_first, w_second, w_third, lon_counts, group_list):
    field_count, levels, rows, lon = fields.shape
    group = field_count * levels
    lev_total = remap_weight.shape[0]
    feats = group * n_lev
    hid = w_first.shape[1]
    group_list = group_list.T
    halves = group // 8
    hbm = pl.BlockSpec(memory_space=pltpu.HBM)
    vmem = pl.BlockSpec(memory_space=pltpu.VMEM)
    plane = (8, lon)
    halo = (2 * halves + 2,) + plane
    return pl.pallas_call(
        functools.partial(kernel, n_lat, n_lev, x_size, lev_total),
        out_shape=jax.ShapeDtypeStruct((field_count * lev_total * rows, SLOT), BF),
        in_specs=[hbm, hbm, hbm, hbm, hbm, hbm, hbm, hbm],
        out_specs=vmem,
        scratch_shapes=[
            pltpu.VMEM(halo, F32), pltpu.VMEM(halo, F32),
            pltpu.VMEM(halo, F32), pltpu.VMEM(halo, F32),
            pltpu.VMEM((lon // SLOT, group * rows, SLOT), F32),
            pltpu.VMEM((lon // SLOT, 2 * levels * rows, SLOT), F32),
            pltpu.VMEM((rows, halves) + plane, F32),
            pltpu.VMEM((rows,) + plane, F32), pltpu.VMEM((rows,) + plane, F32),
            pltpu.VMEM((rows + 2,) + plane, F32), pltpu.VMEM((rows + 2,) + plane, F32),
            pltpu.VMEM((rows + 3,) + plane, F32), pltpu.VMEM((rows + 3,) + plane, F32),
            pltpu.VMEM((rows + 2, halves) + plane, F32),
            pltpu.VMEM((4, lon // SLOT, 2, group, SLOT), BF),
            pltpu.SMEM((1, n_lev), jnp.int32),
            pltpu.VMEM((4, n_lev, group, 2 * SLOT), BF),
            pltpu.VMEM((4, n_lev, group, 2 * SLOT), BF),
            pltpu.VMEM(remap_weight.shape, BF), pltpu.VMEM(w_first.shape, BF),
            pltpu.VMEM(w_second.shape, BF), pltpu.VMEM(w_third.shape, BF),
            pltpu.VMEM((feats, feats), BF), pltpu.VMEM((hid, feats), BF),
            pltpu.VMEM((hid, hid), BF), pltpu.VMEM((feats, hid), BF),
            pltpu.VMEM((feats * rows, SLOT), F32),
            pltpu.SemaphoreType.DMA((2,)), pltpu.SemaphoreType.DMA((2,)),
            pltpu.SemaphoreType.DMA((4,)), pltpu.SemaphoreType.DMA((4,)),
            pltpu.SemaphoreType.DMA((2, 4)), pltpu.SemaphoreType.DMA((2, 4)),
            pltpu.SemaphoreType.DMA((6,)), pltpu.SemaphoreType.DMA((2, lon // SLOT)),
            pltpu.SMEM(lon_counts.shape, jnp.int32), pltpu.VMEM(group_list.shape, jnp.int32),
            *[pltpu.VMEM((lon // SLOT, 2, group, SLOT), BF)] * 8,
        ],
        compiler_params=pltpu.CompilerParams(
            collective_id=0, has_side_effects=True, vmem_limit_bytes=LIMIT
        ),
    )(*(pltpu.with_memory_space_constraint(x, pltpu.HBM) for x in (
        lon_counts, group_list, fields.reshape(group * rows, lon), winds.reshape(2 * levels * rows, lon),
        remap_weight, w_first, w_second, w_third,
    ))).reshape(field_count, lev_total, rows, SLOT)


def solution(mesh):
    n_lat, n_lev = mesh.shape["lat"], mesh.shape["lev"]
    in_specs = (
        P(None, "lev", "lat", None),
        P(None, "lev", "lat", None),
        P(), P(), P(), P(),
        P("lat", None),
        P(),
    )
    return jax.shard_map(
        functools.partial(shards, n_lat, n_lev, X_SIZE),
        mesh=mesh,
        in_specs=in_specs,
        out_specs=P(None, None, "lat", "lev"),
        check_vma=False,
    )
```

```python
import functools

import jax
import jax.numpy as jnp
from jax import lax
from jax.experimental import pallas as pl
from jax.experimental.pallas import tpu as pltpu
from jax.sharding import PartitionSpec as P

DIFFUSION = 0.15
SLOT = 128
X_SIZE = 4
URGENT_FROM = 0
LOW = 2
LIMIT = 48000000
MESH = pl.DeviceIdType.MESH
BF = jnp.bfloat16
F32 = jnp.float32


def kernel(
    n_lat, n_lev, x_size, lev_total,
    cnt_hbm, grp_hbm, fields_hbm, winds_hbm, rw_hbm, w1_hbm, w2_hbm, w3_hbm,
    out_ref,
    up_buf, down_buf, lo_buf, hi_buf,
    tracer, wind_in, sown, ew, nw, ah, bh, ag, bg, pred,
    raw_out, starts, send, recv,
    rw_in, w1_in, w2_in, w3_in, mix, w1t, w2t, w3t, done,
    halo_send, halo_recv, send_sem, recv_sem, raw_send, raw_recv, load_sem, in_sem, cnt_ref, grp_ref, *raw_in,
):
    rows, fields_count = 8, 4
    group = send.shape[2]
    levels = group // fields_count
    halves = group // 8
    lon = fields_hbm.shape[1]
    feats = n_lev * group
    chunks = ((2, 3), (4, 5), (0, 1), (6, 7))

    lat = lax.axis_index("lat")
    me = lax.axis_index("lev")
    up, down = lax.rem(lat + 1, n_lat), lax.rem(lat + n_lat - 1, n_lat)
    z_size = n_lev // x_size
    my_z, my_x = me // x_size, lax.rem(me, x_size)
    reach = z_size // 2 - 1
    plane_at = {d: lax.rem(my_z + z_size + d, z_size) * x_size for d in range(-reach, reach + 1)}
    x_at = [lax.rem(my_x + i, x_size) for i in range(x_size)]

    tiles = lon // SLOT
    columns = [slice(t * SLOT, (t + 1) * SLOT) for t in range(tiles)]
    inputs = []
    for t, part in enumerate(columns):
        cut = pl.ds(t * SLOT, SLOT)
        inputs.append(pltpu.make_async_copy(fields_hbm.at[:, cut], tracer.at[t], in_sem.at[0, t]))
        inputs.append(pltpu.make_async_copy(winds_hbm.at[:, cut], wind_in.at[t], in_sem.at[1, t]))
    for copy in inputs:
        copy.start()

    barrier = pltpu.get_barrier_semaphore()

    def greet(where):
        pl.semaphore_signal(barrier, inc=1, device_id=where, device_id_type=MESH)

    for other in (up, down):
        greet({"lat": other})

    for d in range(1, reach + 1):

        @pl.loop(0, x_size)
        def _(x, d=d):
            greet({"lev": plane_at[d] + x})
            greet({"lev": plane_at[-d] + x})

    for x in x_at[1:]:
        greet({"lev": plane_at[0] + x})

    greeted = 2 + 2 * reach * x_size + x_size - 1

    loads = [
        pltpu.make_async_copy(src, dst, load_sem.at[i])
        for i, (src, dst) in enumerate(
            ((cnt_hbm, cnt_ref), (grp_hbm, grp_ref), (rw_hbm, rw_in), (w1_hbm, w1_in), (w2_hbm, w2_in), (w3_hbm, w3_in))
        )
    ]
    for load in loads:
        load.start()

    def twice(x):
        return jnp.concatenate([x, x], axis=0)

    for t, part in enumerate(columns):
        inputs[2 * t].wait()
        inputs[2 * t + 1].wait()
        for r in range(rows):
            for h in range(halves):
                sown[r, h, :, part] = tracer[t, pl.ds(h * 8 * rows + r, 8, stride=rows), :]
            for which, kept in ((0, ew), (1, nw)):
                kept[r, :, part] = twice(wind_in[t, pl.ds(which * levels * rows + r, levels, stride=rows), :])
    for buf, far, near, order in ((up_buf, 6, 7, (6, 7)), (down_buf, 1, 0, (0, 1))):
        for k, r in enumerate(order):
            for h in range(halves):
                buf[k * halves + h] = sown[r, h]
        buf[2 * halves] = jnp.concatenate([ew[near, :levels], nw[near, :levels]], axis=0)
        buf[2 * halves + 1] = nw[far]

    def value(r, h):
        if r < 0:
            return lo_buf[(r + 2) * halves + h]
        if r >= rows:
            return hi_buf[(r - rows) * halves + h]
        return sown[r, h]

    def east(r):
        if r < 0:
            return twice(lo_buf[2 * halves, :levels])
        if r >= rows:
            return twice(hi_buf[2 * halves, :levels])
        return ew[r]

    def north(r):
        if r == -2:
            return lo_buf[2 * halves + 1]
        if r == -1:
            return twice(lo_buf[2 * halves, levels:])
        if r == rows:
            return twice(hi_buf[2 * halves, levels:])
        if r == rows + 1:
            return hi_buf[2 * halves + 1]
        return nw[r]

    def make_side(r):
        u = east(r)
        c = 0.25 * (pltpu.roll(u, 1, axis=1) + u)
        ah[r + 1] = c + DIFFUSION
        bh[r + 1] = c - DIFFUSION

    def make_face(j):
        c = 0.25 * (north(j - 1) + north(j))
        a, b = c + DIFFUSION, c - DIFFUSION
        if j == 0:
            keep = jnp.where(lat > 0, 1.0, 0.0).astype(F32)
            a, b = a * keep, b * keep
        if j == rows:
            keep = jnp.where(lat < n_lat - 1, 1.0, 0.0).astype(F32)
            a, b = a * keep, b * keep
        ag[j + 1] = a
        bg[j + 1] = b

    def sweep(get, span, emit):
        for h in range(halves):
            face = None
            for r in span:
                here = get(r, h)
                if face is None:
                    face = ag[r + 1] * get(r - 1, h) + bg[r + 1] * here
                after = ag[r + 2] * here + bg[r + 2] * get(r + 1, h)
                side = ah[r + 1] * pltpu.roll(here, 1, axis=1) + bh[r + 1] * here
                change = (face - after) + (side - pltpu.roll(side, lon - 1, axis=1))
                emit(r, h, here, change)
                face = after

    def first_step(r, h, here, change):
        pred[r + 1, h] = here + change

    slot_of = {r: (c, i) for c, pair in enumerate(chunks) for i, r in enumerate(pair)}

    def second_step(r, h, here, change):
        c, i = slot_of[r]
        result = (0.5 * (value(r, h) + here + change)).astype(BF)
        for t, part in enumerate(columns):
            raw_out[c, t, i, 8 * h : 8 * h + 8, :] = result[:, part]

    def guess(r, h):
        return pred[r + 1, h]

    lane = lax.broadcasted_iota(jnp.int32, (group, SLOT), 1)
    last_bit = (tiles - 1).bit_length() - 1
    half = x_size // 2

    def first_slot(way):
        return (0, x_size, x_size * (1 + reach) + half)[way]

    def planes(way):
        return (1, reach + 1, reach + 1)[way]

    def chips(way, j):
        if j < reach:
            return range(x_size)
        return range(half) if way == 1 else range(half, x_size)

    def slot(way, j, x):
        return first_slot(way) + j * x_size + x - (half if way == 2 and j == reach else 0)

    def plane_of(way, j):
        return plane_at[-j if way == 2 else j]

    def source_of(way):
        return plane_at[(0, -1, 1)[way]] + my_x

    def pack(c, way):
        for j in range(planes(way)):
            owners = plane_of(way, j)
            for x in chips(way, j):
                start = starts[0, owners + x]
                tile = start >> 7
                after = (tile + 1) - (tile >> last_bit)
                shift = start & (SLOT - 1)
                back = (SLOT - shift) & (SLOT - 1)
                take = lane < SLOT - shift
                for k in range(2):
                    if way == 0:
                        a, b = raw_out[c, tile, k], raw_out[c, after, k]
                    else:
                        arrived = raw_in[2 * c + way - 1]
                        a, b = arrived[tile, k], arrived[after, k]
                    a, b = pltpu.roll(a, back, axis=1), pltpu.roll(b, back, axis=1)
                    send[c, slot(way, j, x), :, k * SLOT : (k + 1) * SLOT] = jnp.where(take, a, b)

    def slot_copy(c, way, j, x):
        return pltpu.make_async_remote_copy(
            src_ref=send.at[c, slot(way, j, x)],
            dst_ref=recv.at[c, source_of(way)],
            send_sem=send_sem.at[c],
            recv_sem=recv_sem.at[c],
            device_id={"lev": plane_of(way, j) + x},
            device_id_type=MESH,
        )

    def ship_plane(c, way, j):
        span = chips(way, j)
        if j > 0:

            @pl.loop(span[0], span[-1] + 1)
            def _(x):
                slot_copy(c, way, j, x).start()

        else:
            for x in x_at[1:]:
                slot_copy(c, way, 0, x).start()

    def ship(c, way):
        order = range(planes(way) - 1, -1, -1)
        if c < URGENT_FROM or way == 0:
            for j in order:
                ship_plane(c, way, j)
        else:
            for first in (True, False):
                for j in order:
                    low = plane_of(way, j) < LOW * x_size
                    pl.when(low if first else jnp.logical_not(low))(functools.partial(ship_plane, c, way, j))

        mine = send.at[c, first_slot(way) + my_x]
        pltpu.make_async_copy(mine, recv.at[c, source_of(way)], recv_sem.at[c]).start()

    def raw_copy(c, w):
        return pltpu.make_async_remote_copy(
            src_ref=raw_out.at[c],
            dst_ref=raw_in[2 * c + w],
            send_sem=raw_send.at[w, c],
            recv_sem=raw_recv.at[w, c],
            device_id={"lev": plane_at[(1, -1)[w]] + my_x},
            device_id_type=MESH,
        )

    def send_raw(c):
        for w in (0, 1):
            raw_copy(c, w).start()

    def relay(c):
        for w in (0, 1):
            raw_copy(c, w).wait_recv()
            pack(c, w + 1)
            ship(c, w + 1)

    def own(c):
        pack(c, 0)
        ship(c, 0)

    for r in range(1, 5):
        make_side(r)
    for j in range(1, 6):
        make_face(j)
    sweep(value, range(1, 5), first_step)
    sweep(guess, (2, 3), second_step)

    pl.semaphore_wait(barrier, greeted)

    halos = [
        pltpu.make_async_remote_copy(
            src_ref=src,
            dst_ref=dst,
            send_sem=halo_send.at[i],
            recv_sem=halo_recv.at[i],
            device_id={"lat": other},
            device_id_type=MESH,
        )
        for i, (src, dst, other) in enumerate(((up_buf, lo_buf, up), (down_buf, hi_buf, down)))
    ]
    for halo in halos:
        halo.start()
    send_raw(0)
    for r in (5, 6):
        make_side(r)
    for j in (6, 7):
        make_face(j)
    sweep(value, (5, 6), first_step)
    sweep(guess, (4, 5), second_step)
    send_raw(1)
    for r in (0, 7):
        make_side(r)
    loads[0].wait()

    def prefix(k, start):
        starts[0, k] = start
        return start + cnt_ref[0, k]

    lax.fori_loop(0, n_lev, prefix, jnp.int32(0))
    own(0)
    own(1)
    relay(0)

    for halo in halos:
        halo.wait()
    for r in (-1, rows):
        make_side(r)
    for j in (-1, 0, rows, rows + 1):
        make_face(j)
    sweep(value, (-1, 0), first_step)
    sweep(guess, (0, 1), second_step)
    send_raw(2)
    sweep(value, (7, 8), first_step)
    sweep(guess, (6, 7), second_step)
    send_raw(3)
    own(2)
    own(3)
    relay(1)

    relay(2)
    relay(3)

    def iota(shape, dim):
        return lax.broadcasted_iota(jnp.int32, shape, dim)

    def hot(mask):
        return jnp.where(mask, 1.0, 0.0).astype(BF)

    def field_of(p):
        return lax.rem(p // levels, fields_count)

    def level_of(p):
        return (p // group) * levels + lax.rem(p, levels)

    def dot(a, b, dims=((1,), (0,))):
        return lax.dot_general(a, b, (dims, ((), ())), preferred_element_type=F32)

    for load in loads[1:]:
        load.wait()
    p_col = iota((feats, feats), 0)
    order = hot(field_of(p_col) * lev_total + level_of(p_col) == iota((feats, feats), 1))
    expand = hot(level_of(iota((feats, lev_total), 0)) == iota((feats, lev_total), 1))
    spread = dot(dot(expand, rw_in[...]).astype(BF), expand, ((1,), (1,)))
    same = field_of(iota((feats, feats), 0)) == field_of(iota((feats, feats), 1))
    mix[...] = jnp.where(same, spread, 0.0).astype(BF)
    w1t[...] = dot(order, w1_in[...]).T.astype(BF)
    w2t[...] = w2_in[...].astype(F32).T.astype(BF)
    w3t[...] = dot(order, w3_in[...].astype(F32).T.astype(BF)).astype(BF)

    def silu(x):
        half = 0.5 * x
        return half + half * jnp.tanh(half)

    for c, pair in enumerate(chunks):
        pltpu.make_async_copy(recv.at[c], recv.at[c], recv_sem.at[c]).wait()
        block = recv[c].reshape(feats, 2 * SLOT)
        remapped = block.astype(F32) + dot(mix[...], block)
        hidden = silu(dot(w1t[...], remapped.astype(BF))).astype(BF)
        hidden = silu(dot(w2t[...], hidden)).astype(BF)
        tendency = dot(w3t[...], hidden).astype(BF).astype(F32)
        for i, r in enumerate(pair):
            hit = jnp.max(jnp.where(grp_ref[...] == lat * rows + r, 1.0, 0.0), keepdims=True)
            part = slice(i * SLOT, (i + 1) * SLOT)
            done[pl.ds(r, feats, stride=rows), :] = remapped[:, part] + hit * tendency[:, part]

    span = levels * rows
    keep = lax.broadcasted_iota(jnp.int32, (span, SLOT), 1) < cnt_ref[0, me]

    def finish(src, carry):
        for f in range(fields_count):
            part = done[pl.ds(pl.multiple_of((src * fields_count + f) * span, span), span), :]
            where = pl.multiple_of((f * n_lev + src) * span, span)
            out_ref[pl.ds(where, span), :] = jnp.where(keep, part, 0.0).astype(BF)
        return carry

    lax.fori_loop(0, n_lev, finish, 0, unroll=4)

    for c in range(len(chunks)):
        sent = send.at[c, pl.ds(0, n_lev - 3)]
        pltpu.make_async_copy(sent, sent, send_sem.at[c]).wait()
        for w in (0, 1):
            raw_copy(c, w).wait_send()


def shards(n_lat, n_lev, x_size, fields, winds, remap_weight, w_first, w_second, w_third, lon_counts, group_list):
    field_count, levels, rows, lon = fields.shape
    group = field_count * levels
    lev_total = remap_weight.shape[0]
    feats = group * n_lev
    hid = w_first.shape[1]
    group_list = group_list.T
    halves = group // 8
    hbm = pl.BlockSpec(memory_space=pltpu.HBM)
    vmem = pl.BlockSpec(memory_space=pltpu.VMEM)
    plane = (8, lon)
    halo = (2 * halves + 2,) + plane
    return pl.pallas_call(
        functools.partial(kernel, n_lat, n_lev, x_size, lev_total),
        out_shape=jax.ShapeDtypeStruct((field_count * lev_total * rows, SLOT), BF),
        in_specs=[hbm, hbm, hbm, hbm, hbm, hbm, hbm, hbm],
        out_specs=vmem,
        scratch_shapes=[
            pltpu.VMEM(halo, F32), pltpu.VMEM(halo, F32),
            pltpu.VMEM(halo, F32), pltpu.VMEM(halo, F32),
            pltpu.VMEM((lon // SLOT, group * rows, SLOT), F32),
            pltpu.VMEM((lon // SLOT, 2 * levels * rows, SLOT), F32),
            pltpu.VMEM((rows, halves) + plane, F32),
            pltpu.VMEM((rows,) + plane, F32), pltpu.VMEM((rows,) + plane, F32),
            pltpu.VMEM((rows + 2,) + plane, F32), pltpu.VMEM((rows + 2,) + plane, F32),
            pltpu.VMEM((rows + 3,) + plane, F32), pltpu.VMEM((rows + 3,) + plane, F32),
            pltpu.VMEM((rows + 2, halves) + plane, F32),
            pltpu.VMEM((4, lon // SLOT, 2, group, SLOT), BF),
            pltpu.SMEM((1, n_lev), jnp.int32),
            pltpu.VMEM((4, n_lev, group, 2 * SLOT), BF),
            pltpu.VMEM((4, n_lev, group, 2 * SLOT), BF),
            pltpu.VMEM(remap_weight.shape, BF), pltpu.VMEM(w_first.shape, BF),
            pltpu.VMEM(w_second.shape, BF), pltpu.VMEM(w_third.shape, BF),
            pltpu.VMEM((feats, feats), BF), pltpu.VMEM((hid, feats), BF),
            pltpu.VMEM((hid, hid), BF), pltpu.VMEM((feats, hid), BF),
            pltpu.VMEM((feats * rows, SLOT), F32),
            pltpu.SemaphoreType.DMA((2,)), pltpu.SemaphoreType.DMA((2,)),
            pltpu.SemaphoreType.DMA((4,)), pltpu.SemaphoreType.DMA((4,)),
            pltpu.SemaphoreType.DMA((2, 4)), pltpu.SemaphoreType.DMA((2, 4)),
            pltpu.SemaphoreType.DMA((6,)), pltpu.SemaphoreType.DMA((2, lon // SLOT)),
            pltpu.SMEM(lon_counts.shape, jnp.int32), pltpu.VMEM(group_list.shape, jnp.int32),
            *[pltpu.VMEM((lon // SLOT, 2, group, SLOT), BF)] * 8,
        ],
        compiler_params=pltpu.CompilerParams(
            collective_id=0, has_side_effects=True, vmem_limit_bytes=LIMIT
        ),
    )(*(pltpu.with_memory_space_constraint(x, pltpu.HBM) for x in (
        lon_counts, group_list, fields.reshape(group * rows, lon), winds.reshape(2 * levels * rows, lon),
        remap_weight, w_first, w_second, w_third,
    ))).reshape(field_count, lev_total, rows, SLOT)


def solution(mesh):
    n_lat, n_lev = mesh.shape["lat"], mesh.shape["lev"]
    in_specs = (
        P(None, "lev", "lat", None),
        P(None, "lev", "lat", None),
        P(), P(), P(), P(),
        P("lat", None),
        P(),
    )
    return jax.shard_map(
        functools.partial(shards, n_lat, n_lev, X_SIZE),
        mesh=mesh,
        in_specs=in_specs,
        out_specs=P(None, None, "lat", "lev"),
        check_vma=False,
    )
```

```python
import functools

import jax
import jax.numpy as jnp
from jax import lax
from jax.experimental import pallas as pl
from jax.experimental.pallas import tpu as pltpu
from jax.sharding import PartitionSpec as P

DIFFUSION = 0.15
SLOT = 128
X_SIZE = 4
URGENT_FROM = 0
LOW = 2
LIMIT = 48000000
MESH = pl.DeviceIdType.MESH
BF = jnp.bfloat16
F32 = jnp.float32


def kernel(
    n_lat, n_lev, x_size, lev_total,
    cnt_hbm, grp_hbm, fields_hbm, winds_hbm, rw_hbm, w1_hbm, w2_hbm, w3_hbm,
    out_ref,
    up_buf, down_buf, lo_buf, hi_buf,
    tracer, wind_in, sown, ew, nw, ah, bh, ag, bg, pred,
    raw_out, starts, send, recv,
    rw_in, w1_in, w2_in, w3_in, mix, w1t, w2t, w3t, done,
    halo_send, halo_recv, send_sem, recv_sem, raw_send, raw_recv, load_sem, in_sem, cnt_ref, grp_ref, *raw_in,
):
    rows, fields_count = 8, 4
    group = send.shape[2]
    levels = group // fields_count
    halves = group // 8
    lon = fields_hbm.shape[1]
    feats = n_lev * group
    chunks = ((2, 3), (4, 5), (0, 1), (6, 7))

    lat = lax.axis_index("lat")
    me = lax.axis_index("lev")
    up, down = lax.rem(lat + 1, n_lat), lax.rem(lat + n_lat - 1, n_lat)
    z_size = n_lev // x_size
    my_z, my_x = me // x_size, lax.rem(me, x_size)
    reach = z_size // 2 - 1
    plane_at = {d: lax.rem(my_z + z_size + d, z_size) * x_size for d in range(-reach, reach + 1)}
    x_at = [lax.rem(my_x + i, x_size) for i in range(x_size)]

    tiles = lon // SLOT
    columns = [slice(t * SLOT, (t + 1) * SLOT) for t in range(tiles)]
    inputs = []
    for t, part in enumerate(columns):
        cut = pl.ds(t * SLOT, SLOT)
        inputs.append(pltpu.make_async_copy(fields_hbm.at[:, cut], tracer.at[t], in_sem.at[0, t]))
        inputs.append(pltpu.make_async_copy(winds_hbm.at[:, cut], wind_in.at[t], in_sem.at[1, t]))
    for copy in inputs:
        copy.start()

    barrier = pltpu.get_barrier_semaphore()

    def greet(where):
        pl.semaphore_signal(barrier, inc=1, device_id=where, device_id_type=MESH)

    for other in (up, down):
        greet({"lat": other})

    for d in range(1, reach + 1):

        @pl.loop(0, x_size)
        def _(x, d=d):
            greet({"lev": plane_at[d] + x})
            greet({"lev": plane_at[-d] + x})

    for x in x_at[1:]:
        greet({"lev": plane_at[0] + x})

    greeted = 2 + 2 * reach * x_size + x_size - 1

    loads = [
        pltpu.make_async_copy(src, dst, load_sem.at[i])
        for i, (src, dst) in enumerate(
            ((cnt_hbm, cnt_ref), (grp_hbm, grp_ref), (rw_hbm, rw_in), (w1_hbm, w1_in), (w2_hbm, w2_in), (w3_hbm, w3_in))
        )
    ]
    for load in loads:
        load.start()

    def twice(x):
        return jnp.concatenate([x, x], axis=0)

    for t, part in enumerate(columns):
        inputs[2 * t].wait()
        inputs[2 * t + 1].wait()
        for r in range(rows):
            for h in range(halves):
                sown[r, h, :, part] = tracer[t, pl.ds(h * 8 * rows + r, 8, stride=rows), :]
            for which, kept in ((0, ew), (1, nw)):
                kept[r, :, part] = twice(wind_in[t, pl.ds(which * levels * rows + r, levels, stride=rows), :])
    for buf, far, near, order in ((up_buf, 6, 7, (6, 7)), (down_buf, 1, 0, (0, 1))):
        for k, r in enumerate(order):
            for h in range(halves):
                buf[k * halves + h] = sown[r, h]
        buf[2 * halves] = jnp.concatenate([ew[near, :levels], nw[near, :levels]], axis=0)
        buf[2 * halves + 1] = nw[far]

    def value(r, h):
        if r < 0:
            return lo_buf[(r + 2) * halves + h]
        if r >= rows:
            return hi_buf[(r - rows) * halves + h]
        return sown[r, h]

    def east(r):
        if r < 0:
            return twice(lo_buf[2 * halves, :levels])
        if r >= rows:
            return twice(hi_buf[2 * halves, :levels])
        return ew[r]

    def north(r):
        if r == -2:
            return lo_buf[2 * halves + 1]
        if r == -1:
            return twice(lo_buf[2 * halves, levels:])
        if r == rows:
            return twice(hi_buf[2 * halves, levels:])
        if r == rows + 1:
            return hi_buf[2 * halves + 1]
        return nw[r]

    def make_side(r):
        u = east(r)
        c = 0.25 * (pltpu.roll(u, 1, axis=1) + u)
        ah[r + 1] = c + DIFFUSION
        bh[r + 1] = c - DIFFUSION

    def make_face(j):
        c = 0.25 * (north(j - 1) + north(j))
        a, b = c + DIFFUSION, c - DIFFUSION
        if j == 0:
            keep = jnp.where(lat > 0, 1.0, 0.0).astype(F32)
            a, b = a * keep, b * keep
        if j == rows:
            keep = jnp.where(lat < n_lat - 1, 1.0, 0.0).astype(F32)
            a, b = a * keep, b * keep
        ag[j + 1] = a
        bg[j + 1] = b

    def sweep(get, span, emit):
        for h in range(halves):
            face = None
            for r in span:
                here = get(r, h)
                if face is None:
                    face = ag[r + 1] * get(r - 1, h) + bg[r + 1] * here
                after = ag[r + 2] * here + bg[r + 2] * get(r + 1, h)
                side = ah[r + 1] * pltpu.roll(here, 1, axis=1) + bh[r + 1] * here
                change = (face - after) + (side - pltpu.roll(side, lon - 1, axis=1))
                emit(r, h, here, change)
                face = after

    def first_step(r, h, here, change):
        pred[r + 1, h] = here + change

    slot_of = {r: (c, i) for c, pair in enumerate(chunks) for i, r in enumerate(pair)}

    def second_step(r, h, here, change):
        c, i = slot_of[r]
        result = (0.5 * (value(r, h) + here + change)).astype(BF)
        for t, part in enumerate(columns):
            raw_out[c, t, i, 8 * h : 8 * h + 8, :] = result[:, part]

    def guess(r, h):
        return pred[r + 1, h]

    lane = lax.broadcasted_iota(jnp.int32, (group, SLOT), 1)
    last_bit = (tiles - 1).bit_length() - 1
    half = x_size // 2

    def first_slot(way):
        return (0, x_size, x_size * (1 + reach) + half)[way]

    def planes(way):
        return (1, reach + 1, reach + 1)[way]

    def chips(way, j):
        if j < reach:
            return range(x_size)
        return range(half) if way == 1 else range(half, x_size)

    def slot(way, j, x):
        return first_slot(way) + j * x_size + x - (half if way == 2 and j == reach else 0)

    def plane_of(way, j):
        return plane_at[-j if way == 2 else j]

    def source_of(way):
        return plane_at[(0, -1, 1)[way]] + my_x

    def pack(c, way):
        for j in range(planes(way)):
            owners = plane_of(way, j)
            for x in chips(way, j):
                start = starts[0, owners + x]
                tile = start >> 7
                after = (tile + 1) - (tile >> last_bit)
                shift = start & (SLOT - 1)
                back = (SLOT - shift) & (SLOT - 1)
                take = lane < SLOT - shift
                for k in range(2):
                    if way == 0:
                        a, b = raw_out[c, tile, k], raw_out[c, after, k]
                    else:
                        arrived = raw_in[2 * c + way - 1]
                        a, b = arrived[tile, k], arrived[after, k]
                    a, b = pltpu.roll(a, back, axis=1), pltpu.roll(b, back, axis=1)
                    send[c, slot(way, j, x), :, k * SLOT : (k + 1) * SLOT] = jnp.where(take, a, b)

    def slot_copy(c, way, j, x):
        return pltpu.make_async_remote_copy(
            src_ref=send.at[c, slot(way, j, x)],
            dst_ref=recv.at[c, source_of(way)],
            send_sem=send_sem.at[c],
            recv_sem=recv_sem.at[c],
            device_id={"lev": plane_of(way, j) + x},
            device_id_type=MESH,
        )

    def ship_plane(c, way, j):
        span = chips(way, j)
        if j > 0:

            @pl.loop(span[0], span[-1] + 1)
            def _(x):
                slot_copy(c, way, j, x).start()

        else:
            for x in x_at[1:]:
                slot_copy(c, way, 0, x).start()

    def ship(c, way):
        order = range(planes(way) - 1, -1, -1)
        if c < URGENT_FROM or way == 0:
            for j in order:
                ship_plane(c, way, j)
        else:
            for first in (True, False):
                for j in order:
                    low = plane_of(way, j) < LOW * x_size
                    pl.when(low if first else jnp.logical_not(low))(functools.partial(ship_plane, c, way, j))

        mine = send.at[c, first_slot(way) + my_x]
        pltpu.make_async_copy(mine, recv.at[c, source_of(way)], recv_sem.at[c]).start()

    def raw_copy(c, w):
        return pltpu.make_async_remote_copy(
            src_ref=raw_out.at[c],
            dst_ref=raw_in[2 * c + w],
            send_sem=raw_send.at[w, c],
            recv_sem=raw_recv.at[w, c],
            device_id={"lev": plane_at[(1, -1)[w]] + my_x},
            device_id_type=MESH,
        )

    def send_raw(c):
        for w in (0, 1):
            raw_copy(c, w).start()

    def relay(c):
        for w in (0, 1):
            raw_copy(c, w).wait_recv()
            pack(c, w + 1)
            ship(c, w + 1)

    def own(c):
        pack(c, 0)
        ship(c, 0)

    for r in range(1, 5):
        make_side(r)
    for j in range(1, 6):
        make_face(j)
    sweep(value, range(1, 5), first_step)
    sweep(guess, (2, 3), second_step)

    pl.semaphore_wait(barrier, greeted)

    halos = [
        pltpu.make_async_remote_copy(
            src_ref=src,
            dst_ref=dst,
            send_sem=halo_send.at[i],
            recv_sem=halo_recv.at[i],
            device_id={"lat": other},
            device_id_type=MESH,
        )
        for i, (src, dst, other) in enumerate(((up_buf, lo_buf, up), (down_buf, hi_buf, down)))
    ]
    send_raw(0)
    for halo in halos:
        halo.start()
    for r in (5, 6):
        make_side(r)
    for j in (6, 7):
        make_face(j)
    sweep(value, (5, 6), first_step)
    sweep(guess, (4, 5), second_step)
    send_raw(1)
    for r in (0, 7):
        make_side(r)
    loads[0].wait()

    def prefix(k, start):
        starts[0, k] = start
        return start + cnt_ref[0, k]

    lax.fori_loop(0, n_lev, prefix, jnp.int32(0))
    own(0)
    own(1)
    relay(0)

    for halo in halos:
        halo.wait()
    for r in (-1, rows):
        make_side(r)
    for j in (-1, 0, rows, rows + 1):
        make_face(j)
    sweep(value, (-1, 0), first_step)
    sweep(guess, (0, 1), second_step)
    send_raw(2)
    sweep(value, (7, 8), first_step)
    sweep(guess, (6, 7), second_step)
    send_raw(3)
    own(2)
    own(3)
    relay(1)

    relay(2)
    relay(3)

    def iota(shape, dim):
        return lax.broadcasted_iota(jnp.int32, shape, dim)

    def hot(mask):
        return jnp.where(mask, 1.0, 0.0).astype(BF)

    def field_of(p):
        return lax.rem(p // levels, fields_count)

    def level_of(p):
        return (p // group) * levels + lax.rem(p, levels)

    def dot(a, b, dims=((1,), (0,))):
        return lax.dot_general(a, b, (dims, ((), ())), preferred_element_type=F32)

    for load in loads[1:]:
        load.wait()
    p_col = iota((feats, feats), 0)
    order = hot(field_of(p_col) * lev_total + level_of(p_col) == iota((feats, feats), 1))
    expand = hot(level_of(iota((feats, lev_total), 0)) == iota((feats, lev_total), 1))
    spread = dot(dot(expand, rw_in[...]).astype(BF), expand, ((1,), (1,)))
    same = field_of(iota((feats, feats), 0)) == field_of(iota((feats, feats), 1))
    mix[...] = jnp.where(same, spread, 0.0).astype(BF)
    w1t[...] = dot(order, w1_in[...]).T.astype(BF)
    w2t[...] = w2_in[...].astype(F32).T.astype(BF)
    w3t[...] = dot(order, w3_in[...].astype(F32).T.astype(BF)).astype(BF)

    def silu(x):
        half = 0.5 * x
        return half + half * jnp.tanh(half)

    for c, pair in enumerate(chunks):
        pltpu.make_async_copy(recv.at[c], recv.at[c], recv_sem.at[c]).wait()
        block = recv[c].reshape(feats, 2 * SLOT)
        remapped = block.astype(F32) + dot(mix[...], block)
        hidden = silu(dot(w1t[...], remapped.astype(BF))).astype(BF)
        hidden = silu(dot(w2t[...], hidden)).astype(BF)
        tendency = dot(w3t[...], hidden).astype(BF).astype(F32)
        for i, r in enumerate(pair):
            hit = jnp.max(jnp.where(grp_ref[...] == lat * rows + r, 1.0, 0.0), keepdims=True)
            part = slice(i * SLOT, (i + 1) * SLOT)
            done[pl.ds(r, feats, stride=rows), :] = remapped[:, part] + hit * tendency[:, part]

    span = levels * rows
    keep = lax.broadcasted_iota(jnp.int32, (span, SLOT), 1) < cnt_ref[0, me]

    def finish(src, carry):
        for f in range(fields_count):
            part = done[pl.ds(pl.multiple_of((src * fields_count + f) * span, span), span), :]
            where = pl.multiple_of((f * n_lev + src) * span, span)
            out_ref[pl.ds(where, span), :] = jnp.where(keep, part, 0.0).astype(BF)
        return carry

    lax.fori_loop(0, n_lev, finish, 0, unroll=4)

    for c in range(len(chunks)):
        sent = send.at[c, pl.ds(0, n_lev - 3)]
        pltpu.make_async_copy(sent, sent, send_sem.at[c]).wait()
        for w in (0, 1):
            raw_copy(c, w).wait_send()


def shards(n_lat, n_lev, x_size, fields, winds, remap_weight, w_first, w_second, w_third, lon_counts, group_list):
    field_count, levels, rows, lon = fields.shape
    group = field_count * levels
    lev_total = remap_weight.shape[0]
    feats = group * n_lev
    hid = w_first.shape[1]
    group_list = group_list.T
    halves = group // 8
    hbm = pl.BlockSpec(memory_space=pltpu.HBM)
    vmem = pl.BlockSpec(memory_space=pltpu.VMEM)
    plane = (8, lon)
    halo = (2 * halves + 2,) + plane
    return pl.pallas_call(
        functools.partial(kernel, n_lat, n_lev, x_size, lev_total),
        out_shape=jax.ShapeDtypeStruct((field_count * lev_total * rows, SLOT), BF),
        in_specs=[hbm, hbm, hbm, hbm, hbm, hbm, hbm, hbm],
        out_specs=vmem,
        scratch_shapes=[
            pltpu.VMEM(halo, F32), pltpu.VMEM(halo, F32),
            pltpu.VMEM(halo, F32), pltpu.VMEM(halo, F32),
            pltpu.VMEM((lon // SLOT, group * rows, SLOT), F32),
            pltpu.VMEM((lon // SLOT, 2 * levels * rows, SLOT), F32),
            pltpu.VMEM((rows, halves) + plane, F32),
            pltpu.VMEM((rows,) + plane, F32), pltpu.VMEM((rows,) + plane, F32),
            pltpu.VMEM((rows + 2,) + plane, F32), pltpu.VMEM((rows + 2,) + plane, F32),
            pltpu.VMEM((rows + 3,) + plane, F32), pltpu.VMEM((rows + 3,) + plane, F32),
            pltpu.VMEM((rows + 2, halves) + plane, F32),
            pltpu.VMEM((4, lon // SLOT, 2, group, SLOT), BF),
            pltpu.SMEM((1, n_lev), jnp.int32),
            pltpu.VMEM((4, n_lev, group, 2 * SLOT), BF),
            pltpu.VMEM((4, n_lev, group, 2 * SLOT), BF),
            pltpu.VMEM(remap_weight.shape, BF), pltpu.VMEM(w_first.shape, BF),
            pltpu.VMEM(w_second.shape, BF), pltpu.VMEM(w_third.shape, BF),
            pltpu.VMEM((feats, feats), BF), pltpu.VMEM((hid, feats), BF),
            pltpu.VMEM((hid, hid), BF), pltpu.VMEM((feats, hid), BF),
            pltpu.VMEM((feats * rows, SLOT), F32),
            pltpu.SemaphoreType.DMA((2,)), pltpu.SemaphoreType.DMA((2,)),
            pltpu.SemaphoreType.DMA((4,)), pltpu.SemaphoreType.DMA((4,)),
            pltpu.SemaphoreType.DMA((2, 4)), pltpu.SemaphoreType.DMA((2, 4)),
            pltpu.SemaphoreType.DMA((6,)), pltpu.SemaphoreType.DMA((2, lon // SLOT)),
            pltpu.SMEM(lon_counts.shape, jnp.int32), pltpu.VMEM(group_list.shape, jnp.int32),
            *[pltpu.VMEM((lon // SLOT, 2, group, SLOT), BF)] * 8,
        ],
        compiler_params=pltpu.CompilerParams(
            collective_id=0, has_side_effects=True, vmem_limit_bytes=LIMIT
        ),
    )(*(pltpu.with_memory_space_constraint(x, pltpu.HBM) for x in (
        lon_counts, group_list, fields.reshape(group * rows, lon), winds.reshape(2 * levels * rows, lon),
        remap_weight, w_first, w_second, w_third,
    ))).reshape(field_count, lev_total, rows, SLOT)


def solution(mesh):
    n_lat, n_lev = mesh.shape["lat"], mesh.shape["lev"]
    in_specs = (
        P(None, "lev", "lat", None),
        P(None, "lev", "lat", None),
        P(), P(), P(), P(),
        P("lat", None),
        P(),
    )
    return jax.shard_map(
        functools.partial(shards, n_lat, n_lev, X_SIZE),
        mesh=mesh,
        in_specs=in_specs,
        out_specs=P(None, None, "lat", "lev"),
        check_vma=False,
    )
```
